128 devices in a mesh: mid: 8 (over x, y_hi), off: 16 (over z, y_lo, core).
Axes of the slice: x: 4, y: 4 (y_hi: 2, y_lo: 2; y = y_hi * 2 + y_lo), z: 4, core: 2. Of those that a mesh axis runs over, the one named last changes fastest.
Arguments:
- bins_data: bfloat16 [16, 64, 2, 2048], P('off', None, None, 'mid'), may hold values from -6 to 6
- operators: bfloat16 [16, 16, 128, 128], P('off'), may hold values from -0.5 to 0.5
- targets: int32 [16, 16], P('off'), may hold values from 0 to 255
- counts: int32 [16], P('off'), may hold values from 1 to 16, 128 in all
- layer_index: int32 [2, 8, 16], P(None, None, 'mid'), may hold values from 0 to 15
- slowness: float32 [2, 16], replicated, may hold values from 0.8 to 1.25
Outputs:
- wavefield: float32 [64, 256, 2, 2048], P('off', None, None, 'mid')
The draws below stay inside these ranges and needn't reach their ends.
Inputs may be any that keep to these rules, and one draw needn't show every extreme that they name: Slots at positions counts[b] and beyond of bin b's list are unused; some bin has all 16 slots live.
All inputs are finite; a program needn't handle non-finite values. No bound on the sum of `counts` on one device may be relied on, other than what follows from the above.
Results may differ from the reference program's by a relative error of at most 0.0003.
Values may be sent and summed in bfloat16 or wider, within the bound.
A program may use at most 128 MiB of HBM per device.

```python
import math
import jax
import jax.numpy as jnp
import numpy as np
from jax import lax

NB = 16
NH = 256
NM = 2048
BLK = 128
ENT = 16
LAYERS = 16
OFFBLK = 32
STEPS = 2
NF = 64


def plant(entries, key, low, top_value):
    extent = entries.shape
    spot = [jax.random.randint(jax.random.fold_in(key, axis), (), 0, extent[axis]) for axis in range(len(extent))]
    entries = entries.at[tuple(spot)].set(low)
    longest = extent.index(max(extent))
    spot[longest] = (spot[longest] + 1) % extent[longest]
    return entries.at[tuple(spot)].set(top_value)


def levels(rng, extent, pieces, least, high):
    factor_of, own = 1.0, jax.random.fold_in(rng, 6)
    for dim, blocks in pieces:
        draws = jnp.exp(jax.random.uniform(jax.random.fold_in(own, dim), (blocks,), jnp.float32, least / len(pieces), high / len(pieces)))
        factor_of = factor_of * jnp.repeat(draws, extent[dim] // blocks).reshape([-1 if axis == dim else 1 for axis in range(len(extent))])
    return factor_of


def split_up(count, total, most, skew):
    portions = [(1 << 20) // math.isqrt(standing ** skew) + 1 for standing in range(2, count + 1)]
    rest, holding = total - most - (count - 1), [1] * (count - 1)
    while rest > 0:
        free = [i for i in range(count - 1) if holding[i] < most]
        whole, left = sum([portions[i] for i in free]), rest
        for i in free:
            more = min(most - holding[i], max(1, left * portions[i] // whole), rest)
            holding[i] = holding[i] + more
            rest = rest - more
    return np.array([most] + holding)


def ragged_sizes(key, count, total, reach, lean):
    if count == 2:
        one = jax.random.randint(key, (), max(1, total - reach), min(reach, total - 1) + 1)
        return jnp.stack([one, total - one])
    tallies = jnp.asarray(split_up(count, total, reach, lean), jnp.int32)
    pairs = (count - 1) // 2
    donor, sink = tallies[1:1 + 2 * pairs:2], tallies[2:2 + 2 * pairs:2]
    slack = jnp.minimum(donor - 1, reach - sink)
    passed = jax.random.randint(jax.random.fold_in(key, 1), (pairs,), 0, 1 << 20) % (slack + 1)
    tallies = tallies.at[1:1 + 2 * pairs:2].set(donor - passed).at[2:2 + 2 * pairs:2].set(sink + passed)
    return tallies[jax.random.permutation(jax.random.fold_in(key, 2), count)]


def gaussian(own_key, dims, spread, limit, shards=(), kind=jnp.bfloat16):
    array = jax.random.normal(own_key, dims, jnp.float32) * spread
    if len(shards) > 0:
        array = levels(own_key, dims, shards, -0.22, 0.18) * array
    return jnp.clip(array, min=-limit, max=limit).astype(kind)


def setup_inputs(seed: int = 0) -> dict:
    key_of = jax.random.split(jax.random.key(seed), 7)
    return {
        "bins_data": gaussian(key_of[0], (NB, NF, 2, NM), 1.0, 6.0, ((0, 16), (3, 8))),
        "operators": gaussian(key_of[1], (NB, ENT, BLK, BLK), BLK ** -0.5, 0.5, ((0, 16),)),
        "targets": plant(jax.random.randint(key_of[2], (NB, ENT), 0, NH), jax.random.fold_in(key_of[2], 1), 0, NH - 1).astype(jnp.int32),
        "counts": ragged_sizes(key_of[3], NB, NB * ENT // 2, ENT, 2).astype(jnp.int32),
        "layer_index": plant(jax.random.randint(key_of[4], (STEPS, NH // OFFBLK, NM // BLK), 0, LAYERS), jax.random.fold_in(key_of[4], 1), 0, LAYERS - 1).astype(jnp.int32),
        "slowness": jnp.clip(jax.random.uniform(key_of[5], (STEPS, LAYERS), jnp.float32, 0.8, 1.25), 0.8, 1.25),
    }


dz_cells = 2.0
damping = 0.1

def signed_wave(index, length):
    signed = (index + length // 2) % length - length // 2
    return signed.astype(jnp.float32) * (2.0 * math.pi / length)

def root_pair(level):
    magnitude = jnp.sqrt(level * level + damping * damping)
    larger = jnp.sqrt(0.5 * (magnitude + jnp.abs(level)))
    smaller = damping / (2.0 * larger)
    return (jnp.where(level >= 0, larger, smaller), jnp.where(level >= 0, smaller, larger))

def propagator(omega_sq, mid_wave, offset_wave):
    source = 0.5 * (mid_wave - offset_wave)
    receiver = 0.5 * (mid_wave + offset_wave)
    real_s, imag_s = root_pair(omega_sq - source * source)
    real_r, imag_r = root_pair(omega_sq - receiver * receiver)
    decay = jnp.exp(-dz_cells * (imag_s + imag_r))
    turn = dz_cells * (real_s + real_r)
    return (decay * jnp.cos(turn), decay * jnp.sin(turn))

def apply_block(source, weight_block):
    return jnp.dot(source.reshape(-1, weight_block.shape[0]), weight_block, preferred_element_type=jnp.float32).reshape(source.shape)

def reference(bins_data, operators, targets, counts, layer_index, slowness):
    start_field = jnp.zeros((NF, NH, 2, NM), jnp.float32)

    def add_slot(slot_at, current):
        bin_at = slot_at // ENT
        entry_at = slot_at % ENT
        added = apply_block(bins_data[bin_at], operators[bin_at, entry_at])
        live = (entry_at < counts[bin_at]).astype(jnp.float32)
        return current.at[:, targets[bin_at, entry_at]].add(live * added)
    moved = lax.fori_loop(0, NB * ENT, add_slot, start_field)
    field = moved[:, :, 0] + 1j * moved[:, :, 1]
    omega_values = math.pi * (0.1 + 0.8 * (jnp.arange(NF).astype(jnp.float32) + 0.5) / NF)
    offset_wave = signed_wave(jnp.arange(NH), NH)
    mid_wave = signed_wave(jnp.arange(NM), NM)
    phase_real, phase_imag = propagator((omega_values * omega_values)[:, None, None], mid_wave[None, None, :], offset_wave[None, :, None])
    phase = phase_real + 1j * phase_imag
    for depth_step in range(STEPS):
        spectrum = jnp.fft.fft2(field, axes=(1, 2))
        field = jnp.fft.ifft2(spectrum * phase, axes=(1, 2))
        block_slow = slowness[depth_step][layer_index[depth_step]]
        cell_slow = jnp.repeat(jnp.repeat(block_slow, NH // layer_index.shape[1], 0), BLK, 1)
        turn = 2.0 * dz_cells * omega_values[:, None, None] * (cell_slow - 1.0)[None]
        field = field * (jnp.cos(turn) + 1j * jnp.sin(turn))
    return jnp.stack([jnp.real(field), jnp.imag(field)], 2).astype(jnp.float32)
```

```python
import functools
import math

import jax
import jax.numpy as jnp
import numpy as np
from jax import lax
from jax.experimental import pallas as pl
from jax.experimental.pallas import tpu as pltpu
from jax.sharding import PartitionSpec as P


NF = 64
NH = 256
NM = 2048
BLK = 128
ENT = 16
NB = 16
MID = 8
OFF = 16
DZ = 2.0
DAMP = 0.1
MESH = pl.DeviceIdType.MESH
VM = pl.BlockSpec(memory_space=pltpu.VMEM)
F32 = jnp.float32
BF16 = jnp.bfloat16


def halves(table):
    high = np.asarray(table, np.float32).astype(jnp.bfloat16)
    low = (np.asarray(table, np.float64) - high.astype(np.float64)).astype(np.float32)
    return high, low.astype(jnp.bfloat16)


def offset_tables():
    wave = np.array([(2 * (s - 64) + p) % NH for p in range(2) for s in range(128)])
    place = np.arange(NH)
    angle = 2.0 * np.pi * (np.outer(wave, place) % NH) / NH
    cos, sin = np.cos(angle).reshape(2, 128, NH), np.sin(angle).reshape(2, 128, NH)
    forward = np.zeros((2, 2, 128, 2, NH))
    forward[:, 0, :, 0], forward[:, 0, :, 1] = cos, sin
    forward[:, 1, :, 0], forward[:, 1, :, 1] = -sin, cos
    inverse = np.zeros((2, NH, 2, 2, 128))
    cos_t, sin_t = cos.transpose(2, 0, 1), sin.transpose(2, 0, 1)
    inverse[0, :, :, 0], inverse[0, :, :, 1] = cos_t, -sin_t
    inverse[1, :, :, 0], inverse[1, :, :, 1] = sin_t, cos_t
    return halves(forward.reshape(512, 512)), halves(inverse.reshape(512, 512) / NH)


def midpoint_tables():
    inner = np.arange(128)
    wave = (np.arange(128) + 64) % 128
    angle = 2.0 * np.pi * (np.outer(inner, wave) % 128) / 128
    cos, sin = np.cos(angle), np.sin(angle)
    forward = np.block([[cos, -sin], [sin, cos]])
    inverse = np.block([[cos.T, sin.T], [-sin.T, cos.T]]) / NM
    turn = 2.0 * np.pi * np.outer(np.arange(16), inner) / NM
    twiddle = np.stack([np.cos(turn), np.sin(turn)], 1)
    twiddle = np.broadcast_to(twiddle[:, :, None], (16, 2, 8, 128)).astype(np.float32)
    return halves(forward), halves(inverse), np.ascontiguousarray(twiddle)


def split(x):
    high = x.astype(BF16)
    return high, (x - high.astype(F32)).astype(BF16)


def dot(a, b):
    return jnp.dot(a, b, preferred_element_type=F32)


def dot_table_left(high, low, x):
    x_high, x_low = split(x)
    return dot(high, x_high) + (dot(high, x_low) + dot(low, x_high))


def dot_table_right(x, high, low):
    x_high, x_low = split(x)
    return dot(x_high, high) + (dot(x_low, high) + dot(x_high, low))


def times_root(value, step, sign):
    real, imag = value
    step = step % 16
    if step == 0:
        return value
    if step == 4:
        return (-imag * sign, real * sign)
    half = float(np.sqrt(0.5))
    if step == 2:
        return ((real - sign * imag) * half, (imag + sign * real) * half)
    if step == 6:
        return ((-real - sign * imag) * half, (-imag + sign * real) * half)
    c, s = math.cos(2 * math.pi * step / 16), sign * math.sin(2 * math.pi * step / 16)
    return (real * c - imag * s, real * s + imag * c)


def small_fft(values, sign):
    n = len(values)
    if n == 1:
        return values
    even, odd = small_fft(values[0::2], sign), small_fft(values[1::2], sign)
    odd = [times_root(v, k * (16 // n), sign) for k, v in enumerate(odd)]
    return [(e[0] + o[0], e[1] + o[1]) for e, o in zip(even, odd)] + [
        (e[0] - o[0], e[1] - o[1]) for e, o in zip(even, odd)
    ]


def place_here():
    return lax.axis_index("mid"), lax.axis_index("off")


def pair_barrier():
    j, o = place_here()
    partner = o + 1 - 2 * lax.rem(o, 2)
    barrier = pltpu.get_barrier_semaphore()
    pl.semaphore_signal(barrier, inc=1, device_id=(j, partner), device_id_type=MESH)
    pl.semaphore_wait(barrier, 1)
    return j, partner


def wait_bytes(ref, sem):
    pltpu.make_async_copy(ref, ref, sem).wait()


def scatter_kernel(
    s_ref, row_ref, slow_ref, r_ref, rows_ref, slows_ref, ssem, rsem, msem, nsem, tsem
):
    j, o = place_here()
    me = j * OFF + o
    total = MID * OFF
    barrier = pltpu.get_barrier_semaphore()

    def signal(i, _):
        peer = lax.rem(me + i, total)
        pl.semaphore_signal(
            barrier, inc=1, device_id=(peer // OFF, lax.rem(peer, OFF)), device_id_type=MESH
        )
        return 0

    lax.fori_loop(1, total, signal, 0)
    pl.semaphore_wait(barrier, total - 1)

    own_row = pltpu.make_async_copy(row_ref, rows_ref.at[o], msem)
    own_row.start()
    own_slow = pltpu.make_async_copy(slow_ref, slows_ref.at[j], nsem)
    own_slow.start()

    def send_row(i, _):
        peer = lax.rem(o + i, OFF)
        pltpu.make_async_remote_copy(
            row_ref, rows_ref.at[o], tsem.at[0], msem, device_id=(j, peer), device_id_type=MESH
        ).start()
        return 0

    lax.fori_loop(1, OFF, send_row, 0)

    def send_slow(i, _):
        peer = lax.rem(j + i, MID)
        pltpu.make_async_remote_copy(
            slow_ref, slows_ref.at[j], tsem.at[1], nsem, device_id=(peer, o), device_id_type=MESH
        ).start()
        return 0

    lax.fori_loop(1, MID, send_slow, 0)

    def send(i, _):
        peer_j, peer_o = lax.rem(j + i // OFF, MID), lax.rem(o + lax.rem(i, OFF), OFF)
        pltpu.make_async_remote_copy(
            s_ref.at[peer_j, peer_o],
            r_ref.at[j, :, o],
            ssem,
            rsem,
            device_id=(peer_j, peer_o),
            device_id_type=MESH,
        ).start()
        return 0

    lax.fori_loop(1, total, send, 0)
    pltpu.make_async_copy(s_ref.at[j, o], r_ref.at[j, :, o], rsem).start()

    wait_bytes(rows_ref, msem)
    wait_bytes(slows_ref, nsem)
    wait_bytes(rows_ref.at[pl.ds(0, OFF - 1)], tsem.at[0])
    wait_bytes(slows_ref.at[pl.ds(0, MID - 1)], tsem.at[1])
    wait_bytes(r_ref, rsem)
    wait_bytes(s_ref.at[0, pl.ds(0, OFF - 1)], ssem)
    wait_bytes(s_ref.at[pl.ds(1, MID - 1)], ssem)


def scatter(chunks, row, slow):
    return pl.pallas_call(
        scatter_kernel,
        out_shape=[
            jax.ShapeDtypeStruct((MID, 2, NB, ENT, 128), F32),
            jax.ShapeDtypeStruct((NB, 8, NH), jnp.int32),
            jax.ShapeDtypeStruct((MID, 2, 8, 128), F32),
        ],
        in_specs=[VM] * 3,
        out_specs=[VM] * 3,
        scratch_shapes=[pltpu.SemaphoreType.DMA] * 4 + [pltpu.SemaphoreType.DMA((2,))],
        compiler_params=pltpu.CompilerParams(
            collective_id=0, has_side_effects=True, vmem_limit_bytes=40 << 20
        ),
        name="scatter_slots",
    )(chunks, row, slow)


def send_piece(source, target, place, partner, ssem, rsem):
    j = lax.axis_index("mid")
    copy = pltpu.make_async_remote_copy(
        source, target, ssem, rsem.at[place], device_id=(j, partner), device_id_type=MESH
    )
    copy.start()
    return copy


def to_waves_kernel(high_ref, low_ref, rows_ref, r_ref, q_ref, w_high, w_low, away, ssem, rsem):
    core = lax.rem(lax.axis_index("off"), 2)
    j, partner = pair_barrier()
    row = jnp.sum(rows_ref[:, 0, :], axis=0, keepdims=True) - 1
    pick = (lax.broadcasted_iota(jnp.int32, (NH, NB * ENT), 0) == row).astype(F32).astype(BF16)
    for part in range(2):
        cols = pl.ds(part * NH, NH)
        w_high[:, cols] = dot(high_ref[:, cols], pick).astype(BF16)
        w_low[:, cols] = dot(low_ref[:, cols], pick).astype(BF16)
    copies = []
    for pair in range(MID // 2):
        both = jnp.concatenate(
            [
                jnp.concatenate(
                    [r_ref[2 * pair + q, part].reshape(NB * ENT, 128) for q in range(2)], axis=1
                )
                for part in range(2)
            ],
            axis=0,
        )
        out = dot_table_left(w_high[...], w_low[...], both)
        copies += store_waves(out, pair, core, partner, q_ref, away, ssem, rsem)
    for copy in copies:
        copy.wait()


def store_waves(out, pair, core, partner, q_ref, away, ssem, rsem):
    copies = []
    for q in range(2):
        for part in range(2):
            even = out[part * 128 : (part + 1) * 128, q * 128 : (q + 1) * 128]
            odd = out[256 + part * 128 : 256 + (part + 1) * 128, q * 128 : (q + 1) * 128]
            q_ref[core, part, 2 * pair + q] = jnp.where(core == 0, even, odd)
            away[part, 2 * pair + q] = jnp.where(core == 0, odd, even)
    where = (slice(None), pl.ds(2 * pair, 2))
    copies.append(
        send_piece(
            away.at[where],
            q_ref.at[(core,) + where],
            pair,
            partner,
            ssem.at[pair],
            rsem,
        )
    )
    return copies


def exchange_call(kernel, name, out, extra, cid, *args):
    return pl.pallas_call(
        kernel,
        out_shape=jax.ShapeDtypeStruct(out, F32),
        in_specs=[VM] * len(args),
        out_specs=VM,
        scratch_shapes=extra + [pltpu.SemaphoreType.DMA((4,))] * 2,
        compiler_params=pltpu.CompilerParams(
            collective_id=cid, has_side_effects=True, vmem_limit_bytes=56 << 20
        ),
        name=name,
    )(*args)


FIELD = (2, 2, MID, 128, 128)


def midpoint_chunk(q_ref, out_ref, phase_ref, tw_ref, fwd, inv, work, at):
    for sub in range(4):
        rows = pl.ds(at + sub * 8, 8)
        values = [
            (q_ref[a % 2, 0, a // 2, rows, :], q_ref[a % 2, 1, a // 2, rows, :]) for a in range(16)
        ]
        values = small_fft(values, -1)
        for k, (real, imag) in enumerate(values):
            cos, sin = tw_ref[k, 0], tw_ref[k, 1]
            here = pl.ds(k * 32 + sub * 8, 8)
            work[here, 0:128] = real * cos + imag * sin
            work[here, 128:256] = imag * cos - real * sin
    for k in range(16):
        here = pl.ds(k * 32, 32)
        z = dot_table_right(work[here, :], fwd[0][...], fwd[1][...])
        real, imag = z[:, :128], z[:, 128:]
        turn_r = phase_ref[0, k, pl.ds(at, 32), :]
        turn_i = phase_ref[1, k, pl.ds(at, 32), :]
        z = jnp.concatenate(
            [real * turn_r - imag * turn_i, real * turn_i + imag * turn_r], axis=1
        )
        work[here, :] = dot_table_right(z, inv[0][...], inv[1][...])
    for sub in range(4):
        rows = pl.ds(at + sub * 8, 8)
        values = []
        for k in range(16):
            here = pl.ds(k * 32 + sub * 8, 8)
            real, imag = work[here, 0:128], work[here, 128:256]
            cos, sin = tw_ref[k, 0], tw_ref[k, 1]
            values.append((real * cos - imag * sin, real * sin + imag * cos))
        values = small_fft(values, 1)
        for a, (real, imag) in enumerate(values):
            out_ref[a % 2, 0, a // 2, rows, :] = real
            out_ref[a % 2, 1, a // 2, rows, :] = imag


def midpoints_kernel(
    q_ref, phase_ref, tw_ref, fh, fl, ih, il, v_ref, work, done, ssem, rsem
):
    core = lax.rem(lax.axis_index("off"), 2)
    j, partner = pair_barrier()

    def piece(i, start):
        rows = pl.ds(pl.multiple_of(i * 32, 32), 32)
        copy = pltpu.make_async_remote_copy(
            done.at[1 - core, :, :, rows],
            v_ref.at[core, :, :, rows],
            ssem.at[i],
            rsem.at[i],
            device_id=(j, partner),
            device_id_type=MESH,
        )
        copy.start() if start else copy.wait()

    def chunk(i, _):
        at = pl.multiple_of(i * 32, 32)
        midpoint_chunk(q_ref, done, phase_ref, tw_ref, (fh, fl), (ih, il), work, at)
        piece(i, True)
        rows = pl.ds(at, 32)
        v_ref[core, :, :, rows] = done[core, :, :, rows]
        return 0

    lax.fori_loop(0, 4, chunk, 0)

    def finish(i, _):
        piece(i, False)
        return 0

    lax.fori_loop(0, 4, finish, 0)


def space_kernel(
    v_ref, slows_ref, omega_ref, fh, fl, ih, il, q_ref, away, ssem, rsem
):
    core = lax.rem(lax.axis_index("off"), 2)
    j, partner = pair_barrier()
    omega = omega_ref[...]
    copies = []
    for pair in range(MID // 2):
        both = jnp.concatenate(
            [
                jnp.concatenate([v_ref[p, part, 2 * pair + q] for q in range(2)], axis=1)
                for p in range(2)
                for part in range(2)
            ],
            axis=0,
        )
        field = dot_table_left(ih[...], il[...], both)
        turned = []
        for q in range(2):
            turn = 2.0 * DZ * omega * (slows_ref[2 * pair + q, core] - 1.0)
            cos, sin = jnp.cos(turn), jnp.sin(turn)
            lanes = slice(q * 128, (q + 1) * 128)
            out_r, out_i = [], []
            for h in range(8):
                real = field[h * 32 : (h + 1) * 32, lanes]
                imag = field[NH + h * 32 : NH + (h + 1) * 32, lanes]
                c, s = cos[h : h + 1], sin[h : h + 1]
                out_r.append(real * c - imag * s)
                out_i.append(real * s + imag * c)
            turned.append(jnp.concatenate(out_r + out_i, axis=0))
        out = dot_table_left(fh[...], fl[...], jnp.concatenate(turned, axis=1))
        copies += store_waves(out, pair, core, partner, q_ref, away, ssem, rsem)
    for copy in copies:
        copy.wait()


def deliver_kernel(
    q_ref, phase_ref, tw_ref, fh, fl, ih, il, z_ref, work, done, ssem, rsem, lsem
):
    j, o = place_here()
    core = lax.rem(o, 2)
    group = o // 2
    owner = j // 4
    mine = lax.rem(j, 4)
    stays = owner == core
    barrier = pltpu.get_barrier_semaphore()
    for i in range(MID):
        for c in range(2):

            @pl.when(jnp.logical_not(jnp.logical_and(i == j, c == core)))
            def _():
                pl.semaphore_signal(
                    barrier, inc=1, device_id=(i, 2 * group + c), device_id_type=MESH
                )

    pl.semaphore_wait(barrier, 2 * MID - 1)

    def send(i, rows):
        def to(d, _):
            peer = lax.rem(j + d, MID)
            for c in range(2):
                for part in range(2):
                    pltpu.make_async_remote_copy(
                        done.at[c, part, peer, rows],
                        z_ref.at[mine, core, part, c, rows],
                        ssem,
                        rsem,
                        device_id=(peer, 2 * group + owner),
                        device_id_type=MESH,
                    ).start()
            return 0

        lax.fori_loop(1, MID, to, 0)

        @pl.when(jnp.logical_not(stays))
        def _():
            to(0, 0)

        @pl.when(stays)
        def _():
            for c in range(2):
                for part in range(2):
                    pltpu.make_async_copy(
                        done.at[c, part, j, rows], z_ref.at[mine, core, part, c, rows], rsem
                    ).start()

    def chunk(i, _):
        at = pl.multiple_of(i * 32, 32)
        midpoint_chunk(q_ref, done, phase_ref, tw_ref, (fh, fl), (ih, il), work, at)
        send(i, pl.ds(at, 32))
        return 0

    lax.fori_loop(0, 4, chunk, 0)
    wait_bytes(z_ref, rsem)
    wait_bytes(done.at[:, :, pl.ds(0, MID - 1)], ssem)

    @pl.when(jnp.logical_not(stays))
    def _():
        wait_bytes(done.at[:, :, 0], ssem)


def table_specs():
    return [VM] * 6


def midpoints(q, phase, twiddle, fwd, inv, cid):
    return exchange_call(
        midpoints_kernel,
        "midpoints",
        FIELD,
        [pltpu.VMEM((512, 256), F32), pltpu.VMEM(FIELD, F32)],
        cid,
        q,
        phase,
        twiddle,
        *fwd,
        *inv,
    )


def deliver(q, phase, twiddle, fwd, inv, cid):
    args = (q, phase, twiddle, *fwd, *inv)
    return pl.pallas_call(
        deliver_kernel,
        out_shape=jax.ShapeDtypeStruct((4, 2, 2, 2, 128, 128), F32),
        in_specs=[VM] * len(args),
        out_specs=VM,
        scratch_shapes=[
            pltpu.VMEM((512, 256), F32),
            pltpu.VMEM(FIELD, F32),
            pltpu.SemaphoreType.DMA,
            pltpu.SemaphoreType.DMA,
            pltpu.SemaphoreType.DMA,
        ],
        compiler_params=pltpu.CompilerParams(
            collective_id=cid, has_side_effects=True, vmem_limit_bytes=56 << 20
        ),
        name="deliver",
    )(*args)


def last_kernel(z_ref, slow_ref, omega_ref, ih, il, out_ref):
    both = jnp.concatenate(
        [
            jnp.concatenate([z_ref[0, p, part, c] for c in range(2)], axis=1)
            for p in range(2)
            for part in range(2)
        ],
        axis=0,
    )
    field = dot_table_left(ih[...], il[...], both)
    omega = omega_ref[0]
    for c in range(2):
        turn = 2.0 * DZ * omega * (slow_ref[c] - 1.0)
        cos, sin = jnp.cos(turn), jnp.sin(turn)
        lanes = slice(c * 128, (c + 1) * 128)
        for h in range(8):
            rows = slice(h * 32, (h + 1) * 32)
            real, imag = field[rows, lanes], field[NH + h * 32 : NH + (h + 1) * 32, lanes]
            co, si = cos[h : h + 1], sin[h : h + 1]
            out_ref[0, rows, 0, lanes] = real * co - imag * si
            out_ref[0, rows, 1, lanes] = real * si + imag * co


def last(z, slow, omega, inv):
    whole = pl.BlockSpec((512, 512), lambda i: (0, 0))
    return pl.pallas_call(
        last_kernel,
        grid=(4,),
        out_shape=jax.ShapeDtypeStruct((4, NH, 2, 256), F32),
        in_specs=[
            pl.BlockSpec((1, 2, 2, 2, 128, 128), lambda i: (i, 0, 0, 0, 0, 0)),
            pl.BlockSpec((2, 8, 128), lambda i: (0, 0, 0)),
            pl.BlockSpec((1, 8, 128), lambda i: (i, 0, 0)),
            whole,
            whole,
        ],
        out_specs=pl.BlockSpec((1, NH, 2, 256), lambda i: (i, 0, 0, 0)),
        compiler_params=pltpu.CompilerParams(vmem_limit_bytes=40 << 20),
        name="last_offsets",
    )(z, slow, omega, *inv)


def one_way(omega_sq, steps):
    wave = steps.astype(F32) * (math.pi / NM)
    level = omega_sq - wave * wave
    magnitude = jnp.sqrt(level * level + DAMP * DAMP)
    larger = jnp.sqrt(0.5 * (magnitude + jnp.abs(level)))
    smaller = DAMP / (2.0 * larger)
    real = jnp.where(level >= 0, larger, smaller)
    imag = jnp.where(level >= 0, smaller, larger)
    decay = jnp.exp(-DZ * imag)
    return jnp.stack([decay * jnp.cos(DZ * real), decay * jnp.sin(DZ * real)])


def phase_kernel(minus_ref, plus_ref, out_ref):
    def one(k, _):
        for q in range(16):
            low = slice(128 - 8 * q, 256 - 8 * q)
            high = slice(8 * q, 8 * q + 128)
            mr, mi = minus_ref[0, k, :, low], minus_ref[1, k, :, low]
            pr, pi = plus_ref[0, k, :, high], plus_ref[1, k, :, high]
            out_ref[0, k, 8 * q : 8 * q + 8, :] = mr * pr - mi * pi
            out_ref[1, k, 8 * q : 8 * q + 8, :] = mr * pi + mi * pr
        return 0

    lax.fori_loop(0, 16, one, 0)


def phase_table(omega, core):
    shape = (16, 8, 256)
    k = lax.broadcasted_iota(jnp.int32, shape, 0)
    i = lax.broadcasted_iota(jnp.int32, shape, 1)
    x = lax.broadcasted_iota(jnp.int32, shape, 2)
    minus = one_way(omega * omega, k - 8 * core - 2048 + 16 * (x - i))
    plus = one_way(omega * omega, k + 8 * core - 2048 + 16 * (x + i))
    return pl.pallas_call(
        phase_kernel,
        out_shape=jax.ShapeDtypeStruct((2, 16, 128, 128), F32),
        in_specs=[VM] * 2,
        out_specs=VM,
        compiler_params=pltpu.CompilerParams(vmem_limit_bytes=40 << 20),
        name="phase_table",
    )(minus, plus)


def frequency(index):
    return math.pi * (0.1 + 0.8 * (index.astype(F32) + 0.5) / NF)


def local(bins_data, operators, targets, counts, layer_index, slowness):
    j, o = place_here()
    group, core = o // 2, lax.rem(o, 2)
    (forward, inverse), (mid_fwd, mid_inv, twiddle) = offset_tables(), midpoint_tables()
    data = bins_data[0].reshape(8, MID, 2, 2, BLK)
    chunks = jnp.einsum("gjrcm,emn->jgcren", data, operators[0], preferred_element_type=F32)
    chunks = chunks.reshape(MID, OFF, 2, ENT, BLK)

    slot = lax.broadcasted_iota(jnp.int32, (8, NB * ENT), 1)
    spread = jnp.tile(targets, (8, NB))
    live = (slot // ENT == o) & (lax.rem(slot, ENT) < counts[0])
    row = jnp.where(live, spread + 1, 0)

    picks = layer_index[:, :, :, None] == lax.broadcasted_iota(jnp.int32, (1, 1, 1, 16), 3)
    slow = jnp.sum(jnp.where(picks, slowness[:, None, None, :], 0.0), axis=3)
    slow = jnp.broadcast_to(slow.transpose(0, 2, 1)[..., None], (2, 2, 8, 128))

    omega = frequency(group * MID + j)
    received, rows, slows = scatter(chunks, row, slow[0])
    phase = phase_table(omega, core)

    waves = exchange_call(
        to_waves_kernel,
        "to_waves",
        FIELD,
        [
            pltpu.VMEM((512, 512), BF16),
            pltpu.VMEM((512, 512), BF16),
            pltpu.VMEM((2, MID, 128, 128), F32),
        ],
        1,
        *forward,
        rows,
        received,
    )
    spectrum = midpoints(waves, phase, twiddle, mid_fwd, mid_inv, 2)
    waves = exchange_call(
        space_kernel,
        "space",
        FIELD,
        [pltpu.VMEM((2, MID, 128, 128), F32)],
        3,
        spectrum,
        slows,
        jnp.full((8, 128), omega, F32),
        *forward,
        *inverse,
    )
    final = deliver(waves, phase, twiddle, mid_fwd, mid_inv, 4)
    own = frequency(o * 4 + lax.broadcasted_iota(jnp.int32, (4, 8, 128), 0))
    return last(final, slow[1], own, inverse)


def solution(mesh):
    in_specs = (
        P("off", None, None, "mid"),
        P("off", None, None, None),
        P("off", None),
        P("off"),
        P(None, None, "mid"),
        P(),
    )
    out_specs = P("off", None, None, "mid")
    return jax.shard_map(local, mesh=mesh, in_specs=in_specs, out_specs=out_specs, check_vma=False)
```

```python
import functools
import math

import jax
import jax.numpy as jnp
import numpy as np
from jax import lax
from jax.experimental import pallas as pl
from jax.experimental.pallas import tpu as pltpu
from jax.sharding import PartitionSpec as P


NF = 64
NH = 256
NM = 2048
BLK = 128
ENT = 16
NB = 16
MID = 8
OFF = 16
DZ = 2.0
DAMP = 0.1
MESH = pl.DeviceIdType.MESH
LEVELS = 32767.0
VM = pl.BlockSpec(memory_space=pltpu.VMEM)
F32 = jnp.float32
BF16 = jnp.bfloat16


def halves(table):
    high = np.asarray(table, np.float32).astype(jnp.bfloat16)
    low = (np.asarray(table, np.float64) - high.astype(np.float64)).astype(np.float32)
    return high, low.astype(jnp.bfloat16)


def offset_tables():
    forward, inverse = [], []
    place = np.arange(128)
    for p in range(2):
        wave = 2 * (np.arange(128) - 64) + p
        angle = 2.0 * np.pi * (np.outer(wave, place) % NH) / NH
        cos, sin = np.cos(angle), np.sin(angle)
        forward.append(np.block([[cos, sin], [-sin, cos]]))
        inverse.append(np.block([[cos.T, -sin.T], [sin.T, cos.T]]) / NH)
    return halves(np.stack(forward)), halves(np.stack(inverse))


def midpoint_tables():
    inner = np.arange(128)
    wave = (np.arange(128) + 64) % 128
    angle = 2.0 * np.pi * (np.outer(inner, wave) % 128) / 128
    cos, sin = np.cos(angle), np.sin(angle)
    forward = np.block([[cos, -sin], [sin, cos]])
    inverse = np.block([[cos.T, sin.T], [-sin.T, cos.T]]) / NM
    turn = 2.0 * np.pi * np.outer(np.arange(16), inner) / NM
    twiddle = np.stack([np.cos(turn), np.sin(turn)], 1)
    twiddle = np.broadcast_to(twiddle[:, :, None], (16, 2, 8, 128)).astype(np.float32)
    return halves(forward), halves(inverse), np.ascontiguousarray(twiddle)


def split(x):
    high = x.astype(BF16)
    return high, (x - high.astype(F32)).astype(BF16)


def dot(a, b):
    return jnp.dot(a, b, preferred_element_type=F32)


def dot_table_left(high, low, x):
    x_high, x_low = split(x)
    return dot(high, x_high) + (dot(high, x_low) + dot(low, x_high))


def dot_table_right(x, high, low):
    x_high, x_low = split(x)
    return dot(x_high, high) + (dot(x_low, high) + dot(x_high, low))


def times_root(value, step, sign):
    real, imag = value
    step = step % 16
    if step == 0:
        return value
    if step == 4:
        return (-imag * sign, real * sign)
    half = float(np.sqrt(0.5))
    if step == 2:
        return ((real - sign * imag) * half, (imag + sign * real) * half)
    if step == 6:
        return ((-real - sign * imag) * half, (-imag + sign * real) * half)
    c, s = math.cos(2 * math.pi * step / 16), sign * math.sin(2 * math.pi * step / 16)
    return (real * c - imag * s, real * s + imag * c)


def small_fft(values, sign):
    n = len(values)
    if n == 1:
        return values
    even, odd = small_fft(values[0::2], sign), small_fft(values[1::2], sign)
    odd = [times_root(v, k * (16 // n), sign) for k, v in enumerate(odd)]
    return [(e[0] + o[0], e[1] + o[1]) for e, o in zip(even, odd)] + [
        (e[0] - o[0], e[1] - o[1]) for e, o in zip(even, odd)
    ]


def place_here():
    return lax.axis_index("mid"), lax.axis_index("off")


def wait_bytes(ref, sem):
    pltpu.make_async_copy(ref, ref, sem).wait()


def code(values, peak):
    return jnp.round(values * (LEVELS / peak)).astype(jnp.int32).astype(jnp.int16)


def decode(codes, scale):
    return codes.astype(jnp.int32).astype(F32) * scale


def peak_of(arrays):
    top = functools.reduce(jnp.maximum, [jnp.abs(a) for a in arrays])
    return jnp.maximum(jnp.max(top, axis=0, keepdims=True), 1e-30)


def one_way(omega_sq, steps):
    wave = steps.astype(F32) * (math.pi / NM)
    level = omega_sq - wave * wave
    magnitude = jnp.sqrt(level * level + DAMP * DAMP)
    larger = jnp.sqrt(0.5 * (magnitude + jnp.abs(level)))
    smaller = DAMP / (2.0 * larger)
    real = jnp.where(level >= 0, larger, smaller)
    imag = jnp.where(level >= 0, smaller, larger)
    decay = jnp.exp(-DZ * imag)
    return decay * jnp.cos(DZ * real), decay * jnp.sin(DZ * real)


def frequency(index):
    return math.pi * (0.1 + 0.8 * (index.astype(F32) + 0.5) / NF)


def fill_phase(phase, omega, core):
    shape = (8, 256)
    i = lax.broadcasted_iota(jnp.int32, shape, 0)
    x = lax.broadcasted_iota(jnp.int32, shape, 1)
    omega_sq = omega * omega

    def one(k, _):
        mr, mi = one_way(omega_sq, k - 8 * core - NM + 16 * (x - i))
        pr, pi = one_way(omega_sq, k + 8 * core - NM + 16 * (x + i))
        for q in range(16):
            low = slice(128 - 8 * q, 256 - 8 * q)
            high = slice(8 * q, 8 * q + 128)
            ar, ai, br, bi = mr[:, low], mi[:, low], pr[:, high], pi[:, high]
            phase[0, k, 8 * q : 8 * q + 8, :] = ar * br - ai * bi
            phase[1, k, 8 * q : 8 * q + 8, :] = ar * bi + ai * br
        return 0

    lax.fori_loop(0, 16, one, 0)


def midpoint_chunk(x_ref, core, store, phase, tw_ref, fwd, inv, work, at):
    for sub in range(4):
        rows = pl.ds(at + sub * 8, 8)
        values = [
            (x_ref[a % 2, core, 0, a // 2, rows, :], x_ref[a % 2, core, 1, a // 2, rows, :])
            for a in range(16)
        ]
        for k, (real, imag) in enumerate(small_fft(values, -1)):
            cos, sin = tw_ref[k, 0], tw_ref[k, 1]
            here = pl.ds(k * 32 + sub * 8, 8)
            work[here, 0:128] = real * cos + imag * sin
            work[here, 128:256] = imag * cos - real * sin
    for part in range(4):
        here = pl.ds(part * 128, 128)
        z = dot_table_right(work[here, :], fwd[0][...], fwd[1][...])
        real, imag = z[:, :128], z[:, 128:]
        ks = pl.ds(part * 4, 4)
        turn_r = phase[0, ks, pl.ds(at, 32), :].reshape(128, 128)
        turn_i = phase[1, ks, pl.ds(at, 32), :].reshape(128, 128)
        z = jnp.concatenate(
            [real * turn_r - imag * turn_i, real * turn_i + imag * turn_r], axis=1
        )
        work[here, :] = dot_table_right(z, inv[0][...], inv[1][...])
    for sub in range(4):
        values = []
        for k in range(16):
            here = pl.ds(k * 32 + sub * 8, 8)
            real, imag = work[here, 0:128], work[here, 128:256]
            cos, sin = tw_ref[k, 0], tw_ref[k, 1]
            values.append((real * cos - imag * sin, real * sin + imag * cos))
        store(sub, small_fft(values, 1))


def field_kernel(
    bins_ref,
    ops_ref,
    row_ref,
    slow_ref,
    oh_ref,
    ol_ref,
    gh_ref,
    gl_ref,
    fh,
    fl,
    ih,
    il,
    tw_ref,
    z_ref,
    zs_ref,
    made,
    sent,
    sent_s,
    held,
    held_s,
    rows,
    slows,
    turns,
    phase,
    w_high,
    w_low,
    x0,
    d0,
    x1,
    work,
    chunk_out,
    coded,
    coded_s,
    ssem,
    rsem,
    msem,
    pair_s,
    pair_r,
):
    j, o = place_here()
    core, group = lax.rem(o, 2), o // 2
    partner = o + 1 - 2 * core
    me, total = j * OFF + o, MID * OFF
    barrier = pltpu.get_barrier_semaphore()

    def signal(i, _):
        peer = lax.rem(me + i, total)
        pl.semaphore_signal(
            barrier, inc=1, device_id=(peer // OFF, lax.rem(peer, OFF)), device_id_type=MESH
        )
        return 0

    lax.fori_loop(1, total, signal, 0)

    for c in range(2):
        source = bins_ref[c].reshape(2 * NF, BLK)
        for e in range(0, ENT, 2):
            out = dot(source, jnp.concatenate([ops_ref[e], ops_ref[e + 1]], axis=1))
            made[c, pl.ds(e * 128, 128), :] = out[:, :BLK]
            made[c, pl.ds(e * 128 + 128, 128), :] = out[:, BLK:]

    pl.semaphore_wait(barrier, total - 1)

    pltpu.make_async_copy(row_ref, rows.at[o], msem.at[0]).start()
    pltpu.make_async_copy(slow_ref, slows.at[j], msem.at[1]).start()

    def send_row(i, _):
        peer = lax.rem(o + i, OFF)
        pltpu.make_async_remote_copy(
            row_ref, rows.at[o], msem.at[2], msem.at[0], device_id=(j, peer), device_id_type=MESH
        ).start()
        return 0

    lax.fori_loop(1, OFF, send_row, 0)

    def send_slow(i, _):
        peer = lax.rem(j + i, MID)
        pltpu.make_async_remote_copy(
            slow_ref, slows.at[j], msem.at[3], msem.at[1], device_id=(peer, o), device_id_type=MESH
        ).start()
        return 0

    lax.fori_loop(1, MID, send_slow, 0)

    def peer_at(i):
        at = lax.rem(i * 45, total)
        return lax.rem(j + at // OFF, MID), lax.rem(o + lax.rem(at, OFF), OFF)

    def encode(i):
        peer_j, peer_o = peer_at(i)
        f, c = 8 * (peer_o // 2) + peer_j, lax.rem(peer_o, 2)
        values = [made[c, pl.ds(part * NF + f, ENT, stride=2 * NF), :] for part in range(2)]
        peak = peak_of(values)
        for part in range(2):
            sent[peer_j, peer_o, part] = code(values[part], peak)
        sent_s[peer_j, peer_o] = peak * (1.0 / LEVELS)

    def send(i):
        peer_j, peer_o = peer_at(i)
        for source, target, at in ((sent, held, 0), (sent_s, held_s, 1)):
            pltpu.make_async_remote_copy(
                source.at[peer_j, peer_o],
                target.at[j, o],
                ssem.at[at],
                rsem.at[at],
                device_id=(peer_j, peer_o),
                device_id_type=MESH,
            ).start()

    encode(0)
    encode(1)

    def go(i, _):
        encode(i)
        send(i - 1)
        return 0

    lax.fori_loop(2, total, go, 0)
    send(total - 1)
    pltpu.make_async_copy(sent.at[j, o], held.at[j, o], rsem.at[0]).start()
    pltpu.make_async_copy(sent_s.at[j, o], held_s.at[j, o], rsem.at[1]).start()

    own_f = lax.broadcasted_iota(jnp.int32, (8, 128), 0) * 0 + (group * MID + j)
    omega = frequency(own_f)
    fill_phase(phase, jnp.concatenate([omega, omega], axis=1), core)
    wait_bytes(slows, msem.at[1])
    for jm in range(MID):
        turn = 2.0 * DZ * omega * (slows[jm, core] - 1.0)
        turns[jm, 0] = jnp.cos(turn)
        turns[jm, 1] = jnp.sin(turn)
    wait_bytes(rows, msem.at[0])
    target = jnp.sum(rows[:, 0, :], axis=0, keepdims=True) - 1
    spot = lax.broadcasted_iota(jnp.int32, (128, NB * ENT), 0)
    first, second = (spot == target).astype(F32), (spot + 128 == target).astype(F32)
    for p in range(2):
        pick = ((first + second) if p == 0 else (first - second)).astype(BF16)
        for part in range(2):
            cols = pl.ds(part * 128, 128)
            at = pl.ds(part * NH, NH)
            w_high[p, :, at] = dot(oh_ref[p, :, cols], pick).astype(BF16)
            w_low[p, :, at] = dot(ol_ref[p, :, cols], pick).astype(BF16)
    wait_bytes(rows.at[pl.ds(0, OFF - 1)], msem.at[2])
    wait_bytes(slows.at[pl.ds(0, MID - 1)], msem.at[3])
    wait_bytes(held_s, rsem.at[1])
    wait_bytes(held, rsem.at[0])

    def pair_copy(ref, pair, step):
        here = ref.at[core, 1 - core, :, pl.ds(2 * pair, 2)]
        return pltpu.make_async_remote_copy(
            here,
            here,
            pair_s.at[step, pair],
            pair_r.at[step, pair],
            device_id=(j, partner),
            device_id_type=MESH,
        )

    def put_waves(ref, pair, p, out):
        for q in range(2):
            for part in range(2):
                ref[core, p, part, 2 * pair + q] = out[
                    part * 128 : (part + 1) * 128, q * 128 : (q + 1) * 128
                ]

    def to_waves(pair, _):
        both = jnp.concatenate(
            [
                jnp.concatenate(
                    [
                        decode(held[2 * pair + q, :, part], held_s[2 * pair + q]).reshape(
                            NB * ENT, 128
                        )
                        for q in range(2)
                    ],
                    axis=1,
                )
                for part in range(2)
            ],
            axis=0,
        )
        for p in range(2):
            put_waves(x0, pair, p, dot_table_left(w_high[p], w_low[p], both))
        pair_copy(x0, pair, 0).start()
        return 0

    lax.fori_loop(0, MID // 2, to_waves, 0)
    for pair in range(MID // 2):
        pair_copy(x0, pair, 0).wait_recv()

    def chunk_copy(i):
        here = d0.at[core, 1 - core, :, :, pl.ds(pl.multiple_of(i * 32, 32), 32)]
        return pltpu.make_async_remote_copy(
            here,
            here,
            pair_s.at[1, i],
            pair_r.at[1, i],
            device_id=(j, partner),
            device_id_type=MESH,
        )

    def first_chunk(i, _):
        at = pl.multiple_of(i * 32, 32)

        def store(sub, values):
            rows_here = pl.ds(at + sub * 8, 8)
            for a, (real, imag) in enumerate(values):
                d0[core, a % 2, 0, a // 2, rows_here, :] = real
                d0[core, a % 2, 1, a // 2, rows_here, :] = imag

        midpoint_chunk(x0, core, store, phase, tw_ref, (fh, fl), (ih, il), work, at)
        chunk_copy(i).start()
        return 0

    lax.fori_loop(0, 4, first_chunk, 0)
    for i in range(4):
        chunk_copy(i).wait_recv()

    def space(pair, _):
        fields = []
        for p in range(2):
            both = jnp.concatenate(
                [
                    jnp.concatenate([d0[p, core, part, 2 * pair + q] for q in range(2)], axis=1)
                    for part in range(2)
                ],
                axis=0,
            )
            fields.append(dot_table_left(gh_ref[p], gl_ref[p], both))
        ends = [fields[0] + fields[1], fields[0] - fields[1]]
        for end in range(2):
            turned = []
            for q in range(2):
                cos, sin = turns[2 * pair + q, 0], turns[2 * pair + q, 1]
                lanes = slice(q * 128, (q + 1) * 128)
                out_r, out_i = [], []
                for h in range(4):
                    real = ends[end][h * 32 : (h + 1) * 32, lanes]
                    imag = ends[end][128 + h * 32 : 128 + (h + 1) * 32, lanes]
                    at = 4 * end + h
                    c, s = cos[at : at + 1], sin[at : at + 1]
                    out_r.append(real * c - imag * s)
                    out_i.append(real * s + imag * c)
                turned.append(jnp.concatenate(out_r + out_i, axis=0))
            ends[end] = jnp.concatenate(turned, axis=1)
        folded = (ends[0] + ends[1], ends[0] - ends[1])
        for p in range(2):
            put_waves(x1, pair, p, dot_table_left(oh_ref[p], ol_ref[p], folded[p]))
        pair_copy(x1, pair, 2).start()
        return 0

    lax.fori_loop(0, MID // 2, space, 0)
    for pair in range(MID // 2):
        pair_copy(x1, pair, 2).wait_recv()

    owner, mine = j // 4, lax.rem(j, 4)
    stays = owner == core
    x_at, y_at = j // 2, lax.rem(j, 2)

    def deliver(peer, i, near):
        for source, target, at in ((coded, z_ref, 2), (coded_s, zs_ref, 3)):
            here, there = source.at[peer, i], target.at[mine, core, i]
            if near:
                pltpu.make_async_copy(here, there, rsem.at[at]).start()
            else:
                pltpu.make_async_remote_copy(
                    here,
                    there,
                    ssem.at[at],
                    rsem.at[at],
                    device_id=(peer, 2 * group + owner),
                    device_id_type=MESH,
                ).start()

    def second_chunk(i, _):
        at = pl.multiple_of(i * 32, 32)

        def store(sub, values):
            rows_here = pl.ds(sub * 8, 8)
            for a, (real, imag) in enumerate(values):
                chunk_out[a // 2, a % 2, 0, rows_here, :] = real
                chunk_out[a // 2, a % 2, 1, rows_here, :] = imag

        midpoint_chunk(x1, core, store, phase, tw_ref, (fh, fl), (ih, il), work, at)

        def encode_peer(peer, _):
            for c in range(2):
                values = [chunk_out[peer, c, part] for part in range(2)]
                peak = peak_of(values)
                for part in range(2):
                    coded[peer, i, c, part] = code(values[part], peak)
                coded_s[peer, i, c] = peak * (1.0 / LEVELS)
            return 0

        lax.fori_loop(0, MID, encode_peer, 0)
        for dx, dy in ((1, 0), (0, 1), (3, 0), (2, 1), (1, 1), (2, 0), (3, 1)):
            peer = 2 * lax.rem(x_at + dx, 4) + lax.rem(y_at + dy, 2)
            deliver(peer, i, False)

        @pl.when(stays)
        def _():
            deliver(j, i, True)

        @pl.when(jnp.logical_not(stays))
        def _():
            deliver(j, i, False)

        return 0

    lax.fori_loop(0, 4, second_chunk, 0)

    for at, ref in ((0, sent), (1, sent_s)):
        wait_bytes(ref.at[0, pl.ds(0, OFF - 1)], ssem.at[at])
        wait_bytes(ref.at[pl.ds(1, MID - 1)], ssem.at[at])
    for i in range(4):
        pair_copy(x0, i, 0).wait_send()
        chunk_copy(i).wait_send()
        pair_copy(x1, i, 2).wait_send()
    for at, ref in ((2, coded), (3, coded_s)):
        wait_bytes(ref.at[pl.ds(0, MID - 1)], ssem.at[at])

        @pl.when(jnp.logical_not(stays))
        def _():
            wait_bytes(ref.at[0], ssem.at[at])

    wait_bytes(zs_ref, rsem.at[3])
    wait_bytes(z_ref, rsem.at[2])


HALVES = (2, 2, 2, MID, 128, 128)


def propagate(*args):
    return pl.pallas_call(
        field_kernel,
        out_shape=[
            jax.ShapeDtypeStruct((4, 2, 4, 2, 2, 32, 128), jnp.int16),
            jax.ShapeDtypeStruct((4, 2, 4, 2, 1, 128), F32),
        ],
        in_specs=[VM] * len(args),
        out_specs=[VM] * 2,
        scratch_shapes=[
            pltpu.VMEM((2, ENT * 2 * NF, BLK), F32),
            pltpu.VMEM((MID, OFF, 2, ENT, BLK), jnp.int16),
            pltpu.VMEM((MID, OFF, 1, BLK), F32),
            pltpu.VMEM((MID, NB, 2, ENT, BLK), jnp.int16),
            pltpu.VMEM((MID, NB, 1, BLK), F32),
            pltpu.VMEM((NB, 8, NB * ENT), jnp.int32),
            pltpu.VMEM((MID, 2, 8, 128), F32),
            pltpu.VMEM((MID, 2, 8, 128), F32),
            pltpu.VMEM((2, 16, 128, 128), F32),
            pltpu.VMEM((2, 256, 512), BF16),
            pltpu.VMEM((2, 256, 512), BF16),
            pltpu.VMEM(HALVES, F32),
            pltpu.VMEM(HALVES, F32),
            pltpu.VMEM(HALVES, F32),
            pltpu.VMEM((512, 256), F32),
            pltpu.VMEM((MID, 2, 2, 32, 128), F32),
            pltpu.VMEM((MID, 4, 2, 2, 32, 128), jnp.int16),
            pltpu.VMEM((MID, 4, 2, 1, 128), F32),
            pltpu.SemaphoreType.DMA((4,)),
            pltpu.SemaphoreType.DMA((4,)),
            pltpu.SemaphoreType.DMA((4,)),
            pltpu.SemaphoreType.DMA((3, 4)),
            pltpu.SemaphoreType.DMA((3, 4)),
        ],
        compiler_params=pltpu.CompilerParams(
            collective_id=0, has_side_effects=True, vmem_limit_bytes=56 << 20
        ),
        name="propagate",
    )(*args)


def last_kernel(z_ref, zs_ref, slow_ref, omega_ref, gh_ref, gl_ref, out_ref):
    fields = []
    for p in range(2):
        both = jnp.concatenate(
            [
                jnp.concatenate(
                    [decode(z_ref[0, p, q, c, part], zs_ref[0, p, q, c]) for c in range(2)],
                    axis=1,
                )
                for part in range(2)
                for q in range(4)
            ],
            axis=0,
        )
        fields.append(dot_table_left(gh_ref[p], gl_ref[p], both))
    ends = [fields[0] + fields[1], fields[0] - fields[1]]
    omega = omega_ref[0]
    for c in range(2):
        turn = 2.0 * DZ * omega * (slow_ref[c] - 1.0)
        cos, sin = jnp.cos(turn), jnp.sin(turn)
        lanes = slice(c * 128, (c + 1) * 128)
        for h in range(8):
            end, at = ends[h // 4], (h % 4) * 32
            rows = slice(h * 32, (h + 1) * 32)
            real, imag = end[at : at + 32, lanes], end[128 + at : 160 + at, lanes]
            co, si = cos[h : h + 1], sin[h : h + 1]
            out_ref[0, rows, 0, lanes] = real * co - imag * si
            out_ref[0, rows, 1, lanes] = real * si + imag * co


def last(z, zs, slow, omega, inv):
    whole = pl.BlockSpec((2, 256, 256), lambda i: (0, 0, 0))
    return pl.pallas_call(
        last_kernel,
        grid=(4,),
        out_shape=jax.ShapeDtypeStruct((4, NH, 2, 256), F32),
        in_specs=[
            pl.BlockSpec((1, 2, 4, 2, 2, 32, 128), lambda i: (i, 0, 0, 0, 0, 0, 0)),
            pl.BlockSpec((1, 2, 4, 2, 1, 128), lambda i: (i, 0, 0, 0, 0, 0)),
            pl.BlockSpec((2, 8, 128), lambda i: (0, 0, 0)),
            pl.BlockSpec((1, 8, 128), lambda i: (i, 0, 0)),
            whole,
            whole,
        ],
        out_specs=pl.BlockSpec((1, NH, 2, 256), lambda i: (i, 0, 0, 0)),
        compiler_params=pltpu.CompilerParams(vmem_limit_bytes=40 << 20),
        name="last_offsets",
    )(z, zs, slow, omega, *inv)


def local(bins_data, operators, targets, counts, layer_index, slowness):
    j, o = place_here()
    (forward, inverse), (mid_fwd, mid_inv, twiddle) = offset_tables(), midpoint_tables()
    bins = bins_data[0].reshape(NF, 2, 2, BLK).transpose(2, 1, 0, 3)

    slot = lax.broadcasted_iota(jnp.int32, (8, NB * ENT), 1)
    spread = jnp.tile(targets, (8, NB))
    live = (slot // ENT == o) & (lax.rem(slot, ENT) < counts[0])
    row = jnp.where(live, spread + 1, 0)

    picks = layer_index[:, :, :, None] == lax.broadcasted_iota(jnp.int32, (1, 1, 1, 16), 3)
    slow = jnp.sum(jnp.where(picks, slowness[:, None, None, :], 0.0), axis=3)
    slow = jnp.broadcast_to(slow.transpose(0, 2, 1)[..., None], (2, 2, 8, 128))

    z, zs = propagate(
        bins, operators[0], row, slow[0], *forward, *inverse, *mid_fwd, *mid_inv, twiddle
    )
    own = frequency(o * 4 + lax.broadcasted_iota(jnp.int32, (4, 8, 128), 0))
    return last(z, zs, slow[1], own, inverse)


def solution(mesh):
    in_specs = (
        P("off", None, None, "mid"),
        P("off", None, None, None),
        P("off", None),
        P("off"),
        P(None, None, "mid"),
        P(),
    )
    out_specs = P("off", None, None, "mid")
    return jax.shard_map(local, mesh=mesh, in_specs=in_specs, out_specs=out_specs, check_vma=False)
```

```python
import functools
import itertools
import math

import jax
import jax.numpy as jnp
import numpy as np
from jax import lax
from jax.experimental import pallas as pl
from jax.experimental.pallas import tpu as pltpu
from jax.sharding import PartitionSpec as P


NF = 64
NH = 256
NM = 2048
BLK = 128
ENT = 16
NB = 16
MID = 8
OFF = 16
DZ = 2.0
DAMP = 0.1
MESH = pl.DeviceIdType.MESH
LEVELS = 32767.0
VM = pl.BlockSpec(memory_space=pltpu.VMEM)
SM = pl.BlockSpec(memory_space=pltpu.SMEM)
ANY = pl.BlockSpec(memory_space=pl.ANY)
F32 = jnp.float32
BF16 = jnp.bfloat16


def halves(table):
    high = np.asarray(table, np.float32).astype(jnp.bfloat16)
    low = (np.asarray(table, np.float64) - high.astype(np.float64)).astype(np.float32)
    return high, low.astype(jnp.bfloat16)


def offset_tables():
    forward, inverse = [], []
    place = np.arange(128)
    for p in range(2):
        wave = 2 * (np.arange(128) - 64) + p
        angle = 2.0 * np.pi * (np.outer(wave, place) % NH) / NH
        cos, sin = np.cos(angle), np.sin(angle)
        forward.append(np.block([[cos, sin], [-sin, cos]]))
        inverse.append(np.block([[cos.T, -sin.T], [sin.T, cos.T]]) / NH)
    return halves(np.stack(forward)), halves(np.stack(inverse))


def midpoint_tables():
    inner = np.arange(128)
    wave = (np.arange(128) + 64) % 128
    angle = 2.0 * np.pi * (np.outer(inner, wave) % 128) / 128
    cos, sin = np.cos(angle), np.sin(angle)
    forward = np.block([[cos, -sin], [sin, cos]])
    inverse = np.block([[cos.T, sin.T], [-sin.T, cos.T]]) / NM
    turn = 2.0 * np.pi * np.outer(np.arange(16), inner) / NM
    twiddle = np.stack([np.cos(turn), np.sin(turn)], 1)
    twiddle = np.broadcast_to(twiddle[:, :, None], (16, 2, 8, 128)).astype(np.float32)
    return halves(forward), halves(inverse), np.ascontiguousarray(twiddle)


def split(x):
    high = x.astype(BF16)
    return high, (x - high.astype(F32)).astype(BF16)


def dot(a, b):
    return jnp.dot(a, b, preferred_element_type=F32)


def dot_table_left(high, low, x):
    x_high, x_low = split(x)
    return dot(high, x_high) + (dot(high, x_low) + dot(low, x_high))


def dot_table_right(x, high, low):
    x_high, x_low = split(x)
    return dot(x_high, high) + (dot(x_low, high) + dot(x_high, low))


def times_root(value, step, sign):
    real, imag = value
    step = step % 16
    if step == 0:
        return value
    if step == 4:
        return (-imag * sign, real * sign)
    half = float(np.sqrt(0.5))
    if step == 2:
        return ((real - sign * imag) * half, (imag + sign * real) * half)
    if step == 6:
        return ((-real - sign * imag) * half, (-imag + sign * real) * half)
    c, s = math.cos(2 * math.pi * step / 16), sign * math.sin(2 * math.pi * step / 16)
    return (real * c - imag * s, real * s + imag * c)


def small_fft(values, sign):
    n = len(values)
    if n == 1:
        return values
    even, odd = small_fft(values[0::2], sign), small_fft(values[1::2], sign)
    odd = [times_root(v, k * (16 // n), sign) for k, v in enumerate(odd)]
    return [(e[0] + o[0], e[1] + o[1]) for e, o in zip(even, odd)] + [
        (e[0] - o[0], e[1] - o[1]) for e, o in zip(even, odd)
    ]


def place_here():
    return lax.axis_index("mid"), lax.axis_index("off")


def wait_bytes(ref, sem):
    pltpu.make_async_copy(ref, ref, sem).wait()


def code(values, peak):
    return jnp.round(values * (LEVELS / peak)).astype(jnp.int32).astype(jnp.int16)


def decode(codes, scale):
    return codes.astype(jnp.int32).astype(F32) * scale


def peak_of(arrays):
    top = functools.reduce(jnp.maximum, [jnp.abs(a) for a in arrays])
    return jnp.maximum(jnp.max(top, axis=0, keepdims=True), 1e-30)


def one_way(omega_sq, steps):
    wave = steps.astype(F32) * (math.pi / NM)
    level = omega_sq - wave * wave
    magnitude = jnp.sqrt(level * level + DAMP * DAMP)
    larger = jnp.sqrt(0.5 * (magnitude + jnp.abs(level)))
    smaller = DAMP / (2.0 * larger)
    real = jnp.where(level >= 0, larger, smaller)
    imag = jnp.where(level >= 0, smaller, larger)
    decay = jnp.exp(-DZ * imag)
    return decay * jnp.cos(DZ * real), decay * jnp.sin(DZ * real)


def slow_tile(layers_ref, slowness_ref, step, c):
    at = lax.broadcasted_iota(jnp.int32, (8, 128), 0)
    tile = jnp.zeros((8, 128), F32)
    for h in range(8):
        tile = jnp.where(at == h, slowness_ref[step, layers_ref[step, c, h]], tile)
    return tile


def frequency(index):
    return math.pi * (0.1 + 0.8 * (index.astype(F32) + 0.5) / NF)


def fill_phase(phase, omega, core):
    shape = (8, 256)
    i = lax.broadcasted_iota(jnp.int32, shape, 0)
    x = lax.broadcasted_iota(jnp.int32, shape, 1)
    omega_sq = omega * omega

    def one(k, _):
        mr, mi = one_way(omega_sq, k - 8 * core - NM + 16 * (x - i))
        pr, pi = one_way(omega_sq, k + 8 * core - NM + 16 * (x + i))
        for q in range(16):
            low = slice(128 - 8 * q, 256 - 8 * q)
            high = slice(8 * q, 8 * q + 128)
            ar, ai, br, bi = mr[:, low], mi[:, low], pr[:, high], pi[:, high]
            phase[0, k, 8 * q : 8 * q + 8, :] = ar * br - ai * bi
            phase[1, k, 8 * q : 8 * q + 8, :] = ar * bi + ai * br
        return 0

    lax.fori_loop(0, 16, one, 0)


def midpoint_chunk(x_ref, core, store, phase, tw_ref, fwd, inv, work, at):
    for sub in range(4):
        rows = pl.ds(at + sub * 8, 8)
        values = [
            (x_ref[a % 2, core, 0, a // 2, rows, :], x_ref[a % 2, core, 1, a // 2, rows, :])
            for a in range(16)
        ]
        for k, (real, imag) in enumerate(small_fft(values, -1)):
            cos, sin = tw_ref[k, 0], tw_ref[k, 1]
            here = pl.ds(k * 32 + sub * 8, 8)
            work[here, 0:128] = real * cos + imag * sin
            work[here, 128:256] = imag * cos - real * sin
    for part in range(4):
        here = pl.ds(part * 128, 128)
        z = dot_table_right(work[here, :], fwd[0][...], fwd[1][...])
        real, imag = z[:, :128], z[:, 128:]
        ks = pl.ds(part * 4, 4)
        turn_r = phase[0, ks, pl.ds(at, 32), :].reshape(128, 128)
        turn_i = phase[1, ks, pl.ds(at, 32), :].reshape(128, 128)
        z = jnp.concatenate(
            [real * turn_r - imag * turn_i, real * turn_i + imag * turn_r], axis=1
        )
        work[here, :] = dot_table_right(z, inv[0][...], inv[1][...])
    for sub in range(4):
        values = []
        for k in range(16):
            here = pl.ds(k * 32 + sub * 8, 8)
            real, imag = work[here, 0:128], work[here, 128:256]
            cos, sin = tw_ref[k, 0], tw_ref[k, 1]
            values.append((real * cos - imag * sin, real * sin + imag * cos))
        store(sub, small_fft(values, 1))


def field_kernel(
    targets_ref,
    counts_ref,
    layers_ref,
    slowness_ref,
    bins_hbm,
    ops_hbm,
    *rest,
):
    tables_hbm, (z_ref, zs_ref), scratch = rest[:9], rest[9:11], rest[11:]
    field_body(
        targets_ref,
        counts_ref,
        layers_ref,
        slowness_ref,
        (bins_hbm, ops_hbm, *tables_hbm),
        scratch[:11],
        z_ref,
        zs_ref,
        *scratch[11:],
    )


def field_body(
    targets_ref,
    counts_ref,
    layers_ref,
    slowness_ref,
    held_far,
    held_near,
    z_ref,
    zs_ref,
    row_ref,
    slow_ref,
    made,
    sent,
    sent_s,
    held,
    held_s,
    rows,
    slows,
    turns,
    phase,
    w_high,
    w_low,
    both_high,
    both_low,
    folded,
    x0,
    d0,
    x1,
    work,
    chunk_out,
    coded,
    coded_s,
    ssem,
    rsem,
    msem,
    pair_s,
    pair_r,
    load_sem,
):
    bins_ref, ops_ref, oh_ref, ol_ref, gh_ref, gl_ref, fh, fl, ih, il, tw_ref = held_near
    loads = [
        pltpu.make_async_copy(far, near, load_sem.at[i])
        for i, (far, near) in enumerate(zip(held_far, held_near))
    ]
    j, o = place_here()
    core, group = lax.rem(o, 2), o // 2
    partner = o + 1 - 2 * core
    me, total = j * OFF + o, MID * OFF
    barrier = pltpu.get_barrier_semaphore()

    def signal(i, _):
        peer = lax.rem(me + i, total)
        pl.semaphore_signal(
            barrier, inc=1, device_id=(peer // OFF, lax.rem(peer, OFF)), device_id_type=MESH
        )
        return 0

    for load in loads[:2]:
        load.start()
    lax.fori_loop(1, total, signal, 0)
    for load in loads[2:]:
        load.start()

    for load in loads[:2]:
        load.wait()
    for c in range(2):
        source = bins_ref[0, :, :, c * BLK : (c + 1) * BLK].reshape(2 * NF, BLK)
        for e in range(0, ENT, 2):
            out = dot(source, jnp.concatenate([ops_ref[0, e], ops_ref[0, e + 1]], axis=1))
            made[c, pl.ds(e * 128, 128), :] = out[:, :BLK]
            made[c, pl.ds(e * 128 + 128, 128), :] = out[:, BLK:]

    lane = lax.broadcasted_iota(jnp.int32, (ENT, NB * ENT), 1)
    spread = (lax.rem(lane, ENT) == lax.broadcasted_iota(jnp.int32, lane.shape, 0)).astype(F32)
    found = dot(
        jnp.broadcast_to((targets_ref[...] + 1).astype(F32), (8, ENT)).astype(BF16),
        spread.astype(BF16),
    )[:1]
    slot = lax.broadcasted_iota(jnp.int32, (1, NB * ENT), 1)
    live = (slot // ENT == o) & (lax.rem(slot, ENT) < counts_ref[0])
    row_ref[...] = jnp.where(live, found, 0.0)
    for c in range(2):
        slow_ref[c] = slow_tile(layers_ref, slowness_ref, 0, c)

    pl.semaphore_wait(barrier, total - 1)

    pltpu.make_async_copy(row_ref, rows.at[o], msem.at[0]).start()
    pltpu.make_async_copy(slow_ref, slows.at[j], msem.at[1]).start()

    def send_row(i, _):
        peer = lax.rem(o + i, OFF)
        pltpu.make_async_remote_copy(
            row_ref, rows.at[o], msem.at[2], msem.at[0], device_id=(j, peer), device_id_type=MESH
        ).start()
        return 0

    lax.fori_loop(1, OFF, send_row, 0)

    def send_slow(i, _):
        peer = lax.rem(j + i, MID)
        pltpu.make_async_remote_copy(
            slow_ref, slows.at[j], msem.at[3], msem.at[1], device_id=(peer, o), device_id_type=MESH
        ).start()
        return 0

    lax.fori_loop(1, MID, send_slow, 0)

    x_at, y_at, z_at = j // 2, 2 * lax.rem(j, 2) + lax.rem(o // 2, 2), o // 4

    def peer_at(classes, i):
        there, rest = [], i // 2
        for at, distance in zip((x_at, y_at, z_at), classes):
            step = 1 + 2 * lax.rem(rest, 2) if distance == 1 else distance
            rest = rest // 2 if distance == 1 else rest
            there.append(lax.rem(at + step, 4))
        x, y, z = there
        return 2 * x + y // 2, 4 * z + 2 * lax.rem(y, 2) + lax.rem(core + i, 2)

    def encode(peer_j, peer_o):
        f, c = 8 * (peer_o // 2) + peer_j, lax.rem(peer_o, 2)
        values = [made[c, pl.ds(2 * f + part, ENT, stride=2 * NF), :] for part in range(2)]
        peak = peak_of(values)
        for part in range(2):
            sent[peer_j, peer_o, part] = code(values[part], peak)
        sent_s[peer_j, peer_o] = peak * (1.0 / LEVELS)

    def send(peer_j, peer_o):
        for source, target, at in ((sent, held, 0), (sent_s, held_s, 1)):
            pltpu.make_async_remote_copy(
                source.at[peer_j, peer_o],
                target.at[j, o],
                ssem.at[at],
                rsem.at[at],
                device_id=(peer_j, peer_o),
                device_id_type=MESH,
            ).start()

    for classes in sorted(itertools.product(range(3), repeat=3), key=lambda d: -sum(d)):
        first = 0 if any(classes) else 1
        members = 2 ** (1 + classes.count(1))

        def encode_one(i, _, classes=classes):
            encode(*peer_at(classes, i))
            return 0

        def send_one(i, _, classes=classes):
            send(*peer_at(classes, i))
            return 0

        lax.fori_loop(0, members, encode_one, 0)
        lax.fori_loop(first, members, send_one, 0)
    pltpu.make_async_copy(sent.at[j, o], held.at[j, o], rsem.at[0]).start()
    pltpu.make_async_copy(sent_s.at[j, o], held_s.at[j, o], rsem.at[1]).start()

    for load in loads[2:]:
        load.wait()

    own_f = lax.broadcasted_iota(jnp.int32, (8, 128), 0) * 0 + (group * MID + j)
    omega = frequency(own_f)
    fill_phase(phase, jnp.concatenate([omega, omega], axis=1), core)
    wait_bytes(slows, msem.at[1])
    for jm in range(MID):
        turn = 2.0 * DZ * omega * (slows[jm, core] - 1.0)
        turns[jm, 0] = jnp.cos(turn)
        turns[jm, 1] = jnp.sin(turn)
    wait_bytes(rows, msem.at[0])
    target = jnp.sum(rows[:, 0, :], axis=0, keepdims=True).astype(jnp.int32) - 1
    spot = lax.broadcasted_iota(jnp.int32, (128, NB * ENT), 0)
    first, second = (spot == target).astype(F32), (spot + 128 == target).astype(F32)
    for p in range(2):
        pick = ((first + second) if p == 0 else (first - second)).astype(BF16)
        for part in range(2):
            cols = pl.ds(part * 128, 128)
            at = pl.ds(part * NH, NH)
            w_high[p, :, at] = dot(oh_ref[p, :, cols], pick).astype(BF16)
            w_low[p, :, at] = dot(ol_ref[p, :, cols], pick).astype(BF16)
    wait_bytes(rows.at[pl.ds(0, OFF - 1)], msem.at[2])
    wait_bytes(slows.at[pl.ds(0, MID - 1)], msem.at[3])
    wait_bytes(held_s, rsem.at[1])
    wait_bytes(held, rsem.at[0])

    def pair_copy(ref, pair, step):
        here = ref.at[core, 1 - core, :, pl.ds(2 * pair, 2)]
        return pltpu.make_async_remote_copy(
            here,
            here,
            pair_s.at[step, pair],
            pair_r.at[step, pair],
            device_id=(j, partner),
            device_id_type=MESH,
        )

    def put_waves(ref, pair, p, out):
        for q in range(2):
            for part in range(2):
                ref[core, p, part, 2 * pair + q] = out[
                    part * 128 : (part + 1) * 128, q * 128 : (q + 1) * 128
                ]

    def slots_to_waves(x_high, x_low, p):
        high, low = w_high[p], w_low[p]
        return dot(high, x_high) + (dot(high, x_low) + dot(low, x_high))

    def to_waves(pair, _):
        both = jnp.concatenate(
            [
                jnp.concatenate(
                    [
                        decode(held[2 * pair + q, :, part], held_s[2 * pair + q]).reshape(
                            NB * ENT, 128
                        )
                        for q in range(2)
                    ],
                    axis=1,
                )
                for part in range(2)
            ],
            axis=0,
        )
        x_high, x_low = split(both)
        both_high[pair], both_low[pair] = x_high, x_low
        put_waves(x0, pair, 1 - core, slots_to_waves(x_high, x_low, 1 - core))
        pair_copy(x0, pair, 0).start()
        return 0

    def to_own_waves(pair, _):
        put_waves(x0, pair, core, slots_to_waves(both_high[pair], both_low[pair], core))
        return 0

    lax.fori_loop(0, MID // 2, to_waves, 0)
    lax.fori_loop(0, MID // 2, to_own_waves, 0)
    for pair in range(MID // 2):
        pair_copy(x0, pair, 0).wait_recv()

    def chunk_copy(i):
        here = d0.at[core, 1 - core, :, :, pl.ds(pl.multiple_of(i * 32, 32), 32)]
        return pltpu.make_async_remote_copy(
            here,
            here,
            pair_s.at[1, i],
            pair_r.at[1, i],
            device_id=(j, partner),
            device_id_type=MESH,
        )

    def first_chunk(i, _):
        at = pl.multiple_of(i * 32, 32)

        def store(sub, values):
            rows_here = pl.ds(at + sub * 8, 8)
            for a, (real, imag) in enumerate(values):
                d0[core, a % 2, 0, a // 2, rows_here, :] = real
                d0[core, a % 2, 1, a // 2, rows_here, :] = imag

        midpoint_chunk(x0, core, store, phase, tw_ref, (fh, fl), (ih, il), work, at)
        chunk_copy(i).start()
        return 0

    lax.fori_loop(0, 4, first_chunk, 0)
    for i in range(4):
        chunk_copy(i).wait_recv()

    own_sign = (1 - 2 * core).astype(F32)

    def space(pair, _):
        fields = []
        for p in range(2):
            both = jnp.concatenate(
                [
                    jnp.concatenate([d0[p, core, part, 2 * pair + q] for q in range(2)], axis=1)
                    for part in range(2)
                ],
                axis=0,
            )
            fields.append(dot_table_left(gh_ref[p], gl_ref[p], both))
        ends = [fields[0] + fields[1], fields[0] - fields[1]]
        for end in range(2):
            turned = []
            for q in range(2):
                cos, sin = turns[2 * pair + q, 0], turns[2 * pair + q, 1]
                lanes = slice(q * 128, (q + 1) * 128)
                out_r, out_i = [], []
                for h in range(4):
                    real = ends[end][h * 32 : (h + 1) * 32, lanes]
                    imag = ends[end][128 + h * 32 : 128 + (h + 1) * 32, lanes]
                    at = 4 * end + h
                    c, s = cos[at : at + 1], sin[at : at + 1]
                    out_r.append(real * c - imag * s)
                    out_i.append(real * s + imag * c)
                turned.append(jnp.concatenate(out_r + out_i, axis=0))
            ends[end] = jnp.concatenate(turned, axis=1)
        folded[pair] = ends[0] + own_sign * ends[1]
        other = dot_table_left(
            oh_ref[1 - core], ol_ref[1 - core], ends[0] - own_sign * ends[1]
        )
        put_waves(x1, pair, 1 - core, other)
        pair_copy(x1, pair, 2).start()
        return 0

    def own_space(pair, _):
        put_waves(x1, pair, core, dot_table_left(oh_ref[core], ol_ref[core], folded[pair]))
        return 0

    lax.fori_loop(0, MID // 2, space, 0)
    lax.fori_loop(0, MID // 2, own_space, 0)
    for pair in range(MID // 2):
        pair_copy(x1, pair, 2).wait_recv()

    owner, mine = j // 4, lax.rem(j, 4)
    stays = owner == core
    half_at = lax.rem(j, 2)

    def deliver(peer, i, near):
        for source, target, at in ((coded, z_ref, 2), (coded_s, zs_ref, 3)):
            here, there = source.at[peer, i], target.at[mine, core, i]
            if near:
                pltpu.make_async_copy(here, there, rsem.at[at]).start()
            else:
                pltpu.make_async_remote_copy(
                    here,
                    there,
                    ssem.at[at],
                    rsem.at[at],
                    device_id=(peer, 2 * group + owner),
                    device_id_type=MESH,
                ).start()

    def second_chunk(i, _):
        at = pl.multiple_of(i * 32, 32)

        def store(sub, values):
            rows_here = pl.ds(sub * 8, 8)
            for a, (real, imag) in enumerate(values):
                chunk_out[a // 2, a % 2, 0, rows_here, :] = real
                chunk_out[a // 2, a % 2, 1, rows_here, :] = imag

        midpoint_chunk(x1, core, store, phase, tw_ref, (fh, fl), (ih, il), work, at)

        def encode_peer(peer, _):
            for c in range(2):
                values = [chunk_out[peer, c, part] for part in range(2)]
                peak = peak_of(values)
                for part in range(2):
                    coded[peer, i, c, part] = code(values[part], peak)
                coded_s[peer, i, c] = peak * (1.0 / LEVELS)
            return 0

        lax.fori_loop(0, MID, encode_peer, 0)
        for dx, dy in ((2, 1), (1, 1), (3, 1), (0, 1), (2, 0), (1, 0), (3, 0)):
            peer = 2 * lax.rem(x_at + dx, 4) + lax.rem(half_at + dy, 2)
            deliver(peer, i, False)

        @pl.when(stays)
        def _():
            deliver(j, i, True)

        @pl.when(jnp.logical_not(stays))
        def _():
            deliver(j, i, False)

        return 0

    lax.fori_loop(0, 4, second_chunk, 0)

    for at, ref in ((0, sent), (1, sent_s)):
        wait_bytes(ref.at[0, pl.ds(0, OFF - 1)], ssem.at[at])
        wait_bytes(ref.at[pl.ds(1, MID - 1)], ssem.at[at])
    for i in range(4):
        pair_copy(x0, i, 0).wait_send()
        chunk_copy(i).wait_send()
        pair_copy(x1, i, 2).wait_send()
    for at, ref in ((2, coded), (3, coded_s)):
        wait_bytes(ref.at[pl.ds(0, MID - 1)], ssem.at[at])

        @pl.when(jnp.logical_not(stays))
        def _():
            wait_bytes(ref.at[0], ssem.at[at])

    wait_bytes(zs_ref, rsem.at[3])
    wait_bytes(z_ref, rsem.at[2])


HALVES = (2, 2, 2, MID, 128, 128)


def propagate(*args):
    return pl.pallas_call(
        field_kernel,
        out_shape=[
            jax.ShapeDtypeStruct((4, 2, 4, 2, 2, 32, 128), jnp.int16),
            jax.ShapeDtypeStruct((4, 2, 4, 2, 1, 128), F32),
        ],
        in_specs=[VM] + [SM] * 3 + [ANY] * (len(args) - 4),
        out_specs=[ANY] * 2,
        scratch_shapes=[pltpu.VMEM(a.shape, a.dtype) for a in args[4:]]
        + [
            pltpu.VMEM((1, NB * ENT), F32),
            pltpu.VMEM((2, 8, 128), F32),
            pltpu.VMEM((2, ENT * 2 * NF, BLK), F32),
            pltpu.VMEM((MID, OFF, 2, ENT, BLK), jnp.int16),
            pltpu.VMEM((MID, OFF, 1, BLK), F32),
            pltpu.VMEM((MID, NB, 2, ENT, BLK), jnp.int16),
            pltpu.VMEM((MID, NB, 1, BLK), F32),
            pltpu.VMEM((NB, 1, NB * ENT), F32),
            pltpu.VMEM((MID, 2, 8, 128), F32),
            pltpu.VMEM((MID, 2, 8, 128), F32),
            pltpu.VMEM((2, 16, 128, 128), F32),
            pltpu.VMEM((2, 256, 512), BF16),
            pltpu.VMEM((2, 256, 512), BF16),
            pltpu.VMEM((4, 512, 256), BF16),
            pltpu.VMEM((4, 512, 256), BF16),
            pltpu.VMEM((4, 256, 256), F32),
            pltpu.VMEM(HALVES, F32),
            pltpu.VMEM(HALVES, F32),
            pltpu.VMEM(HALVES, F32),
            pltpu.VMEM((512, 256), F32),
            pltpu.VMEM((MID, 2, 2, 32, 128), F32),
            pltpu.VMEM((MID, 4, 2, 2, 32, 128), jnp.int16),
            pltpu.VMEM((MID, 4, 2, 1, 128), F32),
            pltpu.SemaphoreType.DMA((4,)),
            pltpu.SemaphoreType.DMA((4,)),
            pltpu.SemaphoreType.DMA((4,)),
            pltpu.SemaphoreType.DMA((3, 4)),
            pltpu.SemaphoreType.DMA((3, 4)),
            pltpu.SemaphoreType.DMA((11,)),
        ],
        compiler_params=pltpu.CompilerParams(
            collective_id=0, has_side_effects=True, vmem_limit_bytes=56 << 20
        ),
        name="propagate",
    )(*args)


def last_kernel(z_ref, zs_ref, layers_ref, slowness_ref, gh_ref, gl_ref, out_ref):
    fields = []
    for p in range(2):
        both = jnp.concatenate(
            [
                jnp.concatenate(
                    [decode(z_ref[0, p, q, c, part], zs_ref[0, p, q, c]) for c in range(2)],
                    axis=1,
                )
                for part in range(2)
                for q in range(4)
            ],
            axis=0,
        )
        fields.append(dot_table_left(gh_ref[p], gl_ref[p], both))
    ends = [fields[0] + fields[1], fields[0] - fields[1]]
    f = lax.axis_index("off") * 4 + pl.program_id(0)
    omega = frequency(lax.broadcasted_iota(jnp.int32, (8, 128), 0) * 0 + f)
    for c in range(2):
        turn = 2.0 * DZ * omega * (slow_tile(layers_ref, slowness_ref, 1, c) - 1.0)
        cos, sin = jnp.cos(turn), jnp.sin(turn)
        lanes = slice(c * 128, (c + 1) * 128)
        for h in range(8):
            end, at = ends[h // 4], (h % 4) * 32
            rows = slice(h * 32, (h + 1) * 32)
            real, imag = end[at : at + 32, lanes], end[128 + at : 160 + at, lanes]
            co, si = cos[h : h + 1], sin[h : h + 1]
            out_ref[0, rows, 0, lanes] = real * co - imag * si
            out_ref[0, rows, 1, lanes] = real * si + imag * co


def last(z, zs, layers, slowness, inv):
    whole = pl.BlockSpec((2, 256, 256), lambda i: (0, 0, 0))
    return pl.pallas_call(
        last_kernel,
        grid=(4,),
        out_shape=jax.ShapeDtypeStruct((4, NH, 2, 256), F32),
        in_specs=[
            pl.BlockSpec((1, 2, 4, 2, 2, 32, 128), lambda i: (i, 0, 0, 0, 0, 0, 0)),
            pl.BlockSpec((1, 2, 4, 2, 1, 128), lambda i: (i, 0, 0, 0, 0, 0)),
            SM,
            SM,
            whole,
            whole,
        ],
        out_specs=pl.BlockSpec((1, NH, 2, 256), lambda i: (i, 0, 0, 0)),
        compiler_params=pltpu.CompilerParams(vmem_limit_bytes=56 << 20),
        name="last_offsets",
    )(z, zs, layers, slowness, *inv)


def local(bins_data, operators, targets, counts, layer_index, slowness):
    (forward, inverse), (mid_fwd, mid_inv, twiddle) = offset_tables(), midpoint_tables()
    layers = layer_index.transpose(0, 2, 1)
    z, zs = propagate(
        targets,
        counts,
        layers,
        slowness,
        bins_data,
        operators,
        *forward,
        *inverse,
        *mid_fwd,
        *mid_inv,
        twiddle,
    )
    return last(z, zs, layers, slowness, inverse)


def solution(mesh):
    in_specs = (
        P("off", None, None, "mid"),
        P("off", None, None, None),
        P("off", None),
        P("off"),
        P(None, None, "mid"),
        P(),
    )
    out_specs = P("off", None, None, "mid")
    return jax.shard_map(local, mesh=mesh, in_specs=in_specs, out_specs=out_specs, check_vma=False)
```

```python
import functools
import itertools
import math

import jax
import jax.numpy as jnp
import numpy as np
from jax import lax
from jax.experimental import pallas as pl
from jax.experimental.pallas import tpu as pltpu
from jax.sharding import PartitionSpec as P


NF = 64
NH = 256
NM = 2048
BLK = 128
ENT = 16
NB = 16
MID = 8
OFF = 16
DZ = 2.0
DAMP = 0.1
MESH = pl.DeviceIdType.MESH
LEVELS = 32767.0
VM = pl.BlockSpec(memory_space=pltpu.VMEM)
SM = pl.BlockSpec(memory_space=pltpu.SMEM)
ANY = pl.BlockSpec(memory_space=pl.ANY)
F32 = jnp.float32
BF16 = jnp.bfloat16


def halves(table):
    high = np.asarray(table, np.float32).astype(jnp.bfloat16)
    low = (np.asarray(table, np.float64) - high.astype(np.float64)).astype(np.float32)
    return high, low.astype(jnp.bfloat16)


def offset_tables():
    forward, inverse = [], []
    place = np.arange(128)
    for p in range(2):
        wave = 2 * (np.arange(128) - 64) + p
        angle = 2.0 * np.pi * (np.outer(wave, place) % NH) / NH
        cos, sin = np.cos(angle), np.sin(angle)
        forward.append(np.block([[cos, sin], [-sin, cos]]))
        inverse.append(np.block([[cos.T, -sin.T], [sin.T, cos.T]]) / NH)
    return halves(np.stack(forward)), halves(np.stack(inverse))


def midpoint_tables():
    inner = np.arange(128)
    wave = (np.arange(128) + 64) % 128
    angle = 2.0 * np.pi * (np.outer(inner, wave) % 128) / 128
    cos, sin = np.cos(angle), np.sin(angle)
    forward = np.block([[cos, -sin], [sin, cos]])
    inverse = np.block([[cos.T, sin.T], [-sin.T, cos.T]]) / NM
    turn = 2.0 * np.pi * np.outer(np.arange(16), inner) / NM
    twiddle = np.stack([np.cos(turn), np.sin(turn)], 1)
    twiddle = np.broadcast_to(twiddle[:, :, None], (16, 2, 8, 128)).astype(np.float32)
    return halves(forward), halves(inverse), np.ascontiguousarray(twiddle)


def split(x):
    high = x.astype(BF16)
    return high, (x - high.astype(F32)).astype(BF16)


def dot(a, b):
    return jnp.dot(a, b, preferred_element_type=F32)


def dot_table_left(high, low, x):
    x_high, x_low = split(x)
    return dot(high, x_high) + (dot(high, x_low) + dot(low, x_high))


def dot_table_right(x, high, low):
    x_high, x_low = split(x)
    return dot(x_high, high) + (dot(x_low, high) + dot(x_high, low))


def times_root(value, step, sign):
    real, imag = value
    step = step % 16
    if step == 0:
        return value
    if step == 4:
        return (-imag * sign, real * sign)
    half = float(np.sqrt(0.5))
    if step == 2:
        return ((real - sign * imag) * half, (imag + sign * real) * half)
    if step == 6:
        return ((-real - sign * imag) * half, (-imag + sign * real) * half)
    c, s = math.cos(2 * math.pi * step / 16), sign * math.sin(2 * math.pi * step / 16)
    return (real * c - imag * s, real * s + imag * c)


def small_fft(values, sign):
    n = len(values)
    if n == 1:
        return values
    even, odd = small_fft(values[0::2], sign), small_fft(values[1::2], sign)
    odd = [times_root(v, k * (16 // n), sign) for k, v in enumerate(odd)]
    return [(e[0] + o[0], e[1] + o[1]) for e, o in zip(even, odd)] + [
        (e[0] - o[0], e[1] - o[1]) for e, o in zip(even, odd)
    ]


def place_here():
    return lax.axis_index("mid"), lax.axis_index("off")


def wait_bytes(ref, sem):
    pltpu.make_async_copy(ref, ref, sem).wait()


def code(values, peak):
    return jnp.round(values * (LEVELS / peak)).astype(jnp.int32).astype(jnp.int16)


def decode(codes, scale):
    return codes.astype(jnp.int32).astype(F32) * scale


def peak_of(arrays):
    top = functools.reduce(jnp.maximum, [jnp.abs(a) for a in arrays])
    return jnp.maximum(jnp.max(top, axis=0, keepdims=True), 1e-30)


def one_way(omega_sq, steps):
    wave = steps.astype(F32) * (math.pi / NM)
    level = omega_sq - wave * wave
    magnitude = jnp.sqrt(level * level + DAMP * DAMP)
    larger = jnp.sqrt(0.5 * (magnitude + jnp.abs(level)))
    smaller = DAMP / (2.0 * larger)
    real = jnp.where(level >= 0, larger, smaller)
    imag = jnp.where(level >= 0, smaller, larger)
    decay = jnp.exp(-DZ * imag)
    return decay * jnp.cos(DZ * real), decay * jnp.sin(DZ * real)


def slow_tile(layers_ref, slowness_ref, step, c):
    at = lax.broadcasted_iota(jnp.int32, (8, 128), 0)
    tile = jnp.zeros((8, 128), F32)
    for h in range(8):
        tile = jnp.where(at == h, slowness_ref[step, layers_ref[step, c, h]], tile)
    return tile


def frequency(index):
    return math.pi * (0.1 + 0.8 * (index.astype(F32) + 0.5) / NF)


def fill_phase(phase, omega, core):
    shape = (8, 256)
    i = lax.broadcasted_iota(jnp.int32, shape, 0)
    x = lax.broadcasted_iota(jnp.int32, shape, 1)
    omega_sq = omega * omega

    def one(k, _):
        mr, mi = one_way(omega_sq, k - 8 * core - NM + 16 * (x - i))
        pr, pi = one_way(omega_sq, k + 8 * core - NM + 16 * (x + i))
        for q in range(16):
            low = slice(128 - 8 * q, 256 - 8 * q)
            high = slice(8 * q, 8 * q + 128)
            ar, ai, br, bi = mr[:, low], mi[:, low], pr[:, high], pi[:, high]
            phase[0, k, 8 * q : 8 * q + 8, :] = ar * br - ai * bi
            phase[1, k, 8 * q : 8 * q + 8, :] = ar * bi + ai * br
        return 0

    lax.fori_loop(0, 16, one, 0)


def midpoint_chunk(x_ref, core, store, phase, tw_ref, fwd, inv, work, at):
    for sub in range(4):
        rows = pl.ds(at + sub * 8, 8)
        values = [
            (x_ref[a % 2, core, 0, a // 2, rows, :], x_ref[a % 2, core, 1, a // 2, rows, :])
            for a in range(16)
        ]
        for k, (real, imag) in enumerate(small_fft(values, -1)):
            cos, sin = tw_ref[k, 0], tw_ref[k, 1]
            here = pl.ds(k * 32 + sub * 8, 8)
            work[here, 0:128] = real * cos + imag * sin
            work[here, 128:256] = imag * cos - real * sin
    for part in range(4):
        here = pl.ds(part * 128, 128)
        z = dot_table_right(work[here, :], fwd[0][...], fwd[1][...])
        real, imag = z[:, :128], z[:, 128:]
        ks = pl.ds(part * 4, 4)
        turn_r = phase[0, ks, pl.ds(at, 32), :].reshape(128, 128)
        turn_i = phase[1, ks, pl.ds(at, 32), :].reshape(128, 128)
        z = jnp.concatenate(
            [real * turn_r - imag * turn_i, real * turn_i + imag * turn_r], axis=1
        )
        work[here, :] = dot_table_right(z, inv[0][...], inv[1][...])
    for sub in range(4):
        values = []
        for k in range(16):
            here = pl.ds(k * 32 + sub * 8, 8)
            real, imag = work[here, 0:128], work[here, 128:256]
            cos, sin = tw_ref[k, 0], tw_ref[k, 1]
            values.append((real * cos - imag * sin, real * sin + imag * cos))
        store(sub, small_fft(values, 1))


def field_kernel(
    targets_ref,
    counts_ref,
    layers_ref,
    slowness_ref,
    bins_hbm,
    ops_hbm,
    *rest,
):
    tables_hbm, (z_ref, zs_ref, turn_ref), scratch = rest[:9], rest[9:12], rest[12:]
    field_body(
        targets_ref,
        counts_ref,
        layers_ref,
        slowness_ref,
        (bins_hbm, ops_hbm, *tables_hbm),
        scratch[:11],
        z_ref,
        zs_ref,
        turn_ref,
        *scratch[11:],
    )


def field_body(
    targets_ref,
    counts_ref,
    layers_ref,
    slowness_ref,
    held_far,
    held_near,
    z_ref,
    zs_ref,
    turn_ref,
    row_ref,
    slow_ref,
    made,
    sent,
    sent_s,
    held,
    held_s,
    rows,
    slows,
    turns,
    phase,
    w_high,
    w_low,
    both_high,
    both_low,
    folded,
    x0,
    d0,
    x1,
    work,
    chunk_out,
    coded,
    coded_s,
    ssem,
    rsem,
    msem,
    pair_s,
    pair_r,
    load_sem,
    last_turns,
):
    bins_ref, ops_ref, oh_ref, ol_ref, gh_ref, gl_ref, fh, fl, ih, il, tw_ref = held_near
    loads = [
        pltpu.make_async_copy(far, near, load_sem.at[i])
        for i, (far, near) in enumerate(zip(held_far, held_near))
    ]
    j, o = place_here()
    core, group = lax.rem(o, 2), o // 2
    partner = o + 1 - 2 * core
    me, total = j * OFF + o, MID * OFF
    barrier = pltpu.get_barrier_semaphore()

    def signal(i, _):
        peer = lax.rem(me + i, total)
        pl.semaphore_signal(
            barrier, inc=1, device_id=(peer // OFF, lax.rem(peer, OFF)), device_id_type=MESH
        )
        return 0

    for load in loads[:2]:
        load.start()
    lax.fori_loop(1, total, signal, 0)
    for load in loads[2:]:
        load.start()

    for load in loads[:2]:
        load.wait()
    for c in range(2):
        source = bins_ref[0, :, :, c * BLK : (c + 1) * BLK].reshape(2 * NF, BLK)
        for e in range(0, ENT, 2):
            out = dot(source, jnp.concatenate([ops_ref[0, e], ops_ref[0, e + 1]], axis=1))
            made[c, pl.ds(e * 128, 128), :] = out[:, :BLK]
            made[c, pl.ds(e * 128 + 128, 128), :] = out[:, BLK:]

    lane = lax.broadcasted_iota(jnp.int32, (ENT, NB * ENT), 1)
    spread = (lax.rem(lane, ENT) == lax.broadcasted_iota(jnp.int32, lane.shape, 0)).astype(F32)
    found = dot(
        jnp.broadcast_to((targets_ref[...] + 1).astype(F32), (8, ENT)).astype(BF16),
        spread.astype(BF16),
    )[:1]
    slot = lax.broadcasted_iota(jnp.int32, (1, NB * ENT), 1)
    live = (slot // ENT == o) & (lax.rem(slot, ENT) < counts_ref[0])
    row_ref[...] = jnp.where(live, found, 0.0)
    for c in range(2):
        slow_ref[c] = slow_tile(layers_ref, slowness_ref, 0, c)

    pl.semaphore_wait(barrier, total - 1)

    pltpu.make_async_copy(row_ref, rows.at[o], msem.at[0]).start()
    pltpu.make_async_copy(slow_ref, slows.at[j], msem.at[1]).start()

    def send_row(i, _):
        peer = lax.rem(o + i, OFF)
        pltpu.make_async_remote_copy(
            row_ref, rows.at[o], msem.at[2], msem.at[0], device_id=(j, peer), device_id_type=MESH
        ).start()
        return 0

    lax.fori_loop(1, OFF, send_row, 0)

    def send_slow(i, _):
        peer = lax.rem(j + i, MID)
        pltpu.make_async_remote_copy(
            slow_ref, slows.at[j], msem.at[3], msem.at[1], device_id=(peer, o), device_id_type=MESH
        ).start()
        return 0

    lax.fori_loop(1, MID, send_slow, 0)

    x_at, y_at, z_at = j // 2, 2 * lax.rem(j, 2) + lax.rem(o // 2, 2), o // 4

    def peer_at(classes, i):
        there, rest = [], i // 2
        for at, distance in zip((x_at, y_at, z_at), classes):
            step = 1 + 2 * lax.rem(rest, 2) if distance == 1 else distance
            rest = rest // 2 if distance == 1 else rest
            there.append(lax.rem(at + step, 4))
        x, y, z = there
        return 2 * x + y // 2, 4 * z + 2 * lax.rem(y, 2) + lax.rem(core + i, 2)

    def encode(peer_j, peer_o):
        f, c = 8 * (peer_o // 2) + peer_j, lax.rem(peer_o, 2)
        values = [made[c, pl.ds(2 * f + part, ENT, stride=2 * NF), :] for part in range(2)]
        peak = peak_of(values)
        for part in range(2):
            sent[peer_j, peer_o, part] = code(values[part], peak)
        sent_s[peer_j, peer_o] = peak * (1.0 / LEVELS)

    def send(peer_j, peer_o):
        for source, target, at in ((sent, held, 0), (sent_s, held_s, 1)):
            pltpu.make_async_remote_copy(
                source.at[peer_j, peer_o],
                target.at[j, o],
                ssem.at[at],
                rsem.at[at],
                device_id=(peer_j, peer_o),
                device_id_type=MESH,
            ).start()

    for classes in sorted(itertools.product(range(3), repeat=3), key=lambda d: -sum(d)):
        first = 0 if any(classes) else 1
        members = 2 ** (1 + classes.count(1))

        def encode_one(i, _, classes=classes):
            encode(*peer_at(classes, i))
            return 0

        def send_one(i, _, classes=classes):
            send(*peer_at(classes, i))
            return 0

        lax.fori_loop(0, members, encode_one, 0)
        lax.fori_loop(first, members, send_one, 0)
    pltpu.make_async_copy(sent.at[j, o], held.at[j, o], rsem.at[0]).start()
    pltpu.make_async_copy(sent_s.at[j, o], held_s.at[j, o], rsem.at[1]).start()

    for load in loads[2:]:
        load.wait()

    own_f = lax.broadcasted_iota(jnp.int32, (8, 128), 0) * 0 + (group * MID + j)
    omega = frequency(own_f)
    fill_phase(phase, jnp.concatenate([omega, omega], axis=1), core)
    for c in range(2):
        slow = slow_tile(layers_ref, slowness_ref, 1, c)
        for f in range(4):
            last_f = lax.broadcasted_iota(jnp.int32, (8, 128), 0) * 0 + (o * 4 + f)
            turn = 2.0 * DZ * frequency(last_f) * (slow - 1.0)
            last_turns[f, c, 0] = jnp.cos(turn)
            last_turns[f, c, 1] = jnp.sin(turn)
    give_turns = pltpu.make_async_copy(last_turns, turn_ref, load_sem.at[11])
    give_turns.start()
    wait_bytes(slows, msem.at[1])
    for jm in range(MID):
        turn = 2.0 * DZ * omega * (slows[jm, core] - 1.0)
        turns[jm, 0] = jnp.cos(turn)
        turns[jm, 1] = jnp.sin(turn)
    wait_bytes(rows, msem.at[0])
    target = jnp.sum(rows[:, 0, :], axis=0, keepdims=True).astype(jnp.int32) - 1
    spot = lax.broadcasted_iota(jnp.int32, (128, NB * ENT), 0)
    first, second = (spot == target).astype(F32), (spot + 128 == target).astype(F32)
    for p in range(2):
        pick = ((first + second) if p == 0 else (first - second)).astype(BF16)
        for part in range(2):
            cols = pl.ds(part * 128, 128)
            at = pl.ds(part * NH, NH)
            w_high[p, :, at] = dot(oh_ref[p, :, cols], pick).astype(BF16)
            w_low[p, :, at] = dot(ol_ref[p, :, cols], pick).astype(BF16)
    wait_bytes(rows.at[pl.ds(0, OFF - 1)], msem.at[2])
    wait_bytes(slows.at[pl.ds(0, MID - 1)], msem.at[3])
    wait_bytes(held_s, rsem.at[1])
    wait_bytes(held, rsem.at[0])

    def pair_copy(ref, pair, step):
        here = ref.at[core, 1 - core, :, pl.ds(2 * pair, 2)]
        return pltpu.make_async_remote_copy(
            here,
            here,
            pair_s.at[step, pair],
            pair_r.at[step, pair],
            device_id=(j, partner),
            device_id_type=MESH,
        )

    def put_waves(ref, pair, p, out):
        for q in range(2):
            for part in range(2):
                ref[core, p, part, 2 * pair + q] = out[
                    part * 128 : (part + 1) * 128, q * 128 : (q + 1) * 128
                ]

    def slots_to_waves(x_high, x_low, p):
        high, low = w_high[p], w_low[p]
        return dot(high, x_high) + (dot(high, x_low) + dot(low, x_high))

    def to_waves(pair, _):
        both = jnp.concatenate(
            [
                jnp.concatenate(
                    [
                        decode(held[2 * pair + q, :, part], held_s[2 * pair + q]).reshape(
                            NB * ENT, 128
                        )
                        for q in range(2)
                    ],
                    axis=1,
                )
                for part in range(2)
            ],
            axis=0,
        )
        x_high, x_low = split(both)
        both_high[pair], both_low[pair] = x_high, x_low
        put_waves(x0, pair, 1 - core, slots_to_waves(x_high, x_low, 1 - core))
        pair_copy(x0, pair, 0).start()
        return 0

    def to_own_waves(pair, _):
        put_waves(x0, pair, core, slots_to_waves(both_high[pair], both_low[pair], core))
        return 0

    lax.fori_loop(0, MID // 2, to_waves, 0)
    lax.fori_loop(0, MID // 2, to_own_waves, 0)
    for pair in range(MID // 2):
        pair_copy(x0, pair, 0).wait_recv()

    def chunk_copy(i):
        here = d0.at[core, 1 - core, :, :, pl.ds(pl.multiple_of(i * 32, 32), 32)]
        return pltpu.make_async_remote_copy(
            here,
            here,
            pair_s.at[1, i],
            pair_r.at[1, i],
            device_id=(j, partner),
            device_id_type=MESH,
        )

    def first_chunk(i, _):
        at = pl.multiple_of(i * 32, 32)

        def store(sub, values):
            rows_here = pl.ds(at + sub * 8, 8)
            for a, (real, imag) in enumerate(values):
                d0[core, a % 2, 0, a // 2, rows_here, :] = real
                d0[core, a % 2, 1, a // 2, rows_here, :] = imag

        midpoint_chunk(x0, core, store, phase, tw_ref, (fh, fl), (ih, il), work, at)
        chunk_copy(i).start()
        return 0

    lax.fori_loop(0, 4, first_chunk, 0)
    for i in range(4):
        chunk_copy(i).wait_recv()

    own_sign = (1 - 2 * core).astype(F32)

    def space(pair, _):
        fields = []
        for p in range(2):
            both = jnp.concatenate(
                [
                    jnp.concatenate([d0[p, core, part, 2 * pair + q] for q in range(2)], axis=1)
                    for part in range(2)
                ],
                axis=0,
            )
            fields.append(dot_table_left(gh_ref[p], gl_ref[p], both))
        ends = [fields[0] + fields[1], fields[0] - fields[1]]
        for end in range(2):
            turned = []
            for q in range(2):
                cos, sin = turns[2 * pair + q, 0], turns[2 * pair + q, 1]
                lanes = slice(q * 128, (q + 1) * 128)
                out_r, out_i = [], []
                for h in range(4):
                    real = ends[end][h * 32 : (h + 1) * 32, lanes]
                    imag = ends[end][128 + h * 32 : 128 + (h + 1) * 32, lanes]
                    at = 4 * end + h
                    c, s = cos[at : at + 1], sin[at : at + 1]
                    out_r.append(real * c - imag * s)
                    out_i.append(real * s + imag * c)
                turned.append(jnp.concatenate(out_r + out_i, axis=0))
            ends[end] = jnp.concatenate(turned, axis=1)
        folded[pair] = ends[0] + own_sign * ends[1]
        other = dot_table_left(
            oh_ref[1 - core], ol_ref[1 - core], ends[0] - own_sign * ends[1]
        )
        put_waves(x1, pair, 1 - core, other)
        pair_copy(x1, pair, 2).start()
        return 0

    def own_space(pair, _):
        put_waves(x1, pair, core, dot_table_left(oh_ref[core], ol_ref[core], folded[pair]))
        return 0

    lax.fori_loop(0, MID // 2, space, 0, unroll=2)
    lax.fori_loop(0, MID // 2, own_space, 0, unroll=2)
    for pair in range(MID // 2):
        pair_copy(x1, pair, 2).wait_recv()

    owner, mine = j // 4, lax.rem(j, 4)
    stays = owner == core
    half_at = lax.rem(j, 2)

    def deliver(peer, i, near):
        for source, target, at in ((coded, z_ref, 2), (coded_s, zs_ref, 3)):
            here, there = source.at[peer, i], target.at[mine, core, i]
            if near:
                pltpu.make_async_copy(here, there, rsem.at[at]).start()
            else:
                pltpu.make_async_remote_copy(
                    here,
                    there,
                    ssem.at[at],
                    rsem.at[at],
                    device_id=(peer, 2 * group + owner),
                    device_id_type=MESH,
                ).start()

    def second_chunk(i, _):
        at = pl.multiple_of(i * 32, 32)

        def store(sub, values):
            rows_here = pl.ds(sub * 8, 8)
            for a, (real, imag) in enumerate(values):
                chunk_out[a // 2, a % 2, 0, rows_here, :] = real
                chunk_out[a // 2, a % 2, 1, rows_here, :] = imag

        midpoint_chunk(x1, core, store, phase, tw_ref, (fh, fl), (ih, il), work, at)

        def encode_peer(peer, _):
            for c in range(2):
                values = [chunk_out[peer, c, part] for part in range(2)]
                peak = peak_of(values)
                for part in range(2):
                    coded[peer, i, c, part] = code(values[part], peak)
                coded_s[peer, i, c] = peak * (1.0 / LEVELS)
            return 0

        lax.fori_loop(0, MID, encode_peer, 0)
        for dx, dy in ((2, 1), (1, 1), (3, 1), (0, 1), (2, 0), (1, 0), (3, 0)):
            peer = 2 * lax.rem(x_at + dx, 4) + lax.rem(half_at + dy, 2)
            deliver(peer, i, False)

        @pl.when(stays)
        def _():
            deliver(j, i, True)

        @pl.when(jnp.logical_not(stays))
        def _():
            deliver(j, i, False)

        return 0

    lax.fori_loop(0, 4, second_chunk, 0)

    give_turns.wait()
    for at, ref in ((0, sent), (1, sent_s)):
        wait_bytes(ref.at[0, pl.ds(0, OFF - 1)], ssem.at[at])
        wait_bytes(ref.at[pl.ds(1, MID - 1)], ssem.at[at])
    for i in range(4):
        pair_copy(x0, i, 0).wait_send()
        chunk_copy(i).wait_send()
        pair_copy(x1, i, 2).wait_send()
    for at, ref in ((2, coded), (3, coded_s)):
        wait_bytes(ref.at[pl.ds(0, MID - 1)], ssem.at[at])

        @pl.when(jnp.logical_not(stays))
        def _():
            wait_bytes(ref.at[0], ssem.at[at])

    wait_bytes(zs_ref, rsem.at[3])
    wait_bytes(z_ref, rsem.at[2])


HALVES = (2, 2, 2, MID, 128, 128)


def propagate(*args):
    return pl.pallas_call(
        field_kernel,
        out_shape=[
            jax.ShapeDtypeStruct((4, 2, 4, 2, 2, 32, 128), jnp.int16),
            jax.ShapeDtypeStruct((4, 2, 4, 2, 1, 128), F32),
            jax.ShapeDtypeStruct((4, 2, 2, 8, 128), F32),
        ],
        in_specs=[VM] + [SM] * 3 + [ANY] * (len(args) - 4),
        out_specs=[ANY] * 3,
        scratch_shapes=[pltpu.VMEM(a.shape, a.dtype) for a in args[4:]]
        + [
            pltpu.VMEM((1, NB * ENT), F32),
            pltpu.VMEM((2, 8, 128), F32),
            pltpu.VMEM((2, ENT * 2 * NF, BLK), F32),
            pltpu.VMEM((MID, OFF, 2, ENT, BLK), jnp.int16),
            pltpu.VMEM((MID, OFF, 1, BLK), F32),
            pltpu.VMEM((MID, NB, 2, ENT, BLK), jnp.int16),
            pltpu.VMEM((MID, NB, 1, BLK), F32),
            pltpu.VMEM((NB, 1, NB * ENT), F32),
            pltpu.VMEM((MID, 2, 8, 128), F32),
            pltpu.VMEM((MID, 2, 8, 128), F32),
            pltpu.VMEM((2, 16, 128, 128), F32),
            pltpu.VMEM((2, 256, 512), BF16),
            pltpu.VMEM((2, 256, 512), BF16),
            pltpu.VMEM((4, 512, 256), BF16),
            pltpu.VMEM((4, 512, 256), BF16),
            pltpu.VMEM((4, 256, 256), F32),
            pltpu.VMEM(HALVES, F32),
            pltpu.VMEM(HALVES, F32),
            pltpu.VMEM(HALVES, F32),
            pltpu.VMEM((512, 256), F32),
            pltpu.VMEM((MID, 2, 2, 32, 128), F32),
            pltpu.VMEM((MID, 4, 2, 2, 32, 128), jnp.int16),
            pltpu.VMEM((MID, 4, 2, 1, 128), F32),
            pltpu.SemaphoreType.DMA((4,)),
            pltpu.SemaphoreType.DMA((4,)),
            pltpu.SemaphoreType.DMA((4,)),
            pltpu.SemaphoreType.DMA((3, 4)),
            pltpu.SemaphoreType.DMA((3, 4)),
            pltpu.SemaphoreType.DMA((12,)),
            pltpu.VMEM((4, 2, 2, 8, 128), F32),
        ],
        compiler_params=pltpu.CompilerParams(
            collective_id=0, has_side_effects=True, vmem_limit_bytes=56 << 20
        ),
        name="propagate",
    )(*args)


def last_kernel(z_ref, zs_ref, turn_ref, gh_ref, gl_ref, out_ref):
    fields = []
    for p in range(2):
        both = jnp.concatenate(
            [
                jnp.concatenate(
                    [decode(z_ref[0, p, q, c, part], zs_ref[0, p, q, c]) for c in range(2)],
                    axis=1,
                )
                for part in range(2)
                for q in range(4)
            ],
            axis=0,
        )
        fields.append(dot_table_left(gh_ref[p], gl_ref[p], both))
    ends = [fields[0] + fields[1], fields[0] - fields[1]]
    for c in range(2):
        cos, sin = turn_ref[0, c, 0], turn_ref[0, c, 1]
        lanes = slice(c * 128, (c + 1) * 128)
        for h in range(8):
            end, at = ends[h // 4], (h % 4) * 32
            real, imag = end[at : at + 32, lanes], end[128 + at : 160 + at, lanes]
            co, si = cos[h : h + 1], sin[h : h + 1]
            for part, value in enumerate((real * co - imag * si, real * si + imag * co)):
                out_ref[0, pl.ds(128 * h + 2 * c + part, 32, stride=4), :] = value


def last(z, zs, turns, inv):
    whole = pl.BlockSpec((2, 256, 256), lambda i: (0, 0, 0))
    return pl.pallas_call(
        last_kernel,
        grid=(4,),
        out_shape=jax.ShapeDtypeStruct((4, NH * 4, 128), F32),
        in_specs=[
            pl.BlockSpec((1, 2, 4, 2, 2, 32, 128), lambda i: (i, 0, 0, 0, 0, 0, 0)),
            pl.BlockSpec((1, 2, 4, 2, 1, 128), lambda i: (i, 0, 0, 0, 0, 0)),
            pl.BlockSpec((1, 2, 2, 8, 128), lambda i: (i, 0, 0, 0, 0)),
            whole,
            whole,
        ],
        out_specs=pl.BlockSpec((1, NH * 4, 128), lambda i: (i, 0, 0)),
        compiler_params=pltpu.CompilerParams(vmem_limit_bytes=56 << 20),
        name="last_offsets",
    )(z, zs, turns, *inv)


def local(bins_data, operators, targets, counts, layer_index, slowness):
    (forward, inverse), (mid_fwd, mid_inv, twiddle) = offset_tables(), midpoint_tables()
    layers = layer_index.transpose(0, 2, 1)
    z, zs, turns = propagate(
        targets,
        counts,
        layers,
        slowness,
        bins_data,
        operators,
        *forward,
        *inverse,
        *mid_fwd,
        *mid_inv,
        twiddle,
    )
    rows = last(z, zs, turns, inverse)
    return rows.reshape(4, NH, 2, 2, 128).transpose(0, 1, 3, 2, 4).reshape(4, NH, 2, 256)


def solution(mesh):
    in_specs = (
        P("off", None, None, "mid"),
        P("off", None, None, None),
        P("off", None),
        P("off"),
        P(None, None, "mid"),
        P(),
    )
    out_specs = P("off", None, None, "mid")
    return jax.shard_map(local, mesh=mesh, in_specs=in_specs, out_specs=out_specs, check_vma=False)
```

```python
import functools
import itertools
import math

import jax
import jax.numpy as jnp
import numpy as np
from jax import lax
from jax.experimental import pallas as pl
from jax.experimental.pallas import tpu as pltpu
from jax.sharding import PartitionSpec as P


NF = 64
NH = 256
NM = 2048
BLK = 128
ENT = 16
NB = 16
MID = 8
OFF = 16
DZ = 2.0
DAMP = 0.1
MESH = pl.DeviceIdType.MESH
LEVELS = 32767.0
VM = pl.BlockSpec(memory_space=pltpu.VMEM)
SM = pl.BlockSpec(memory_space=pltpu.SMEM)
ANY = pl.BlockSpec(memory_space=pl.ANY)
F32 = jnp.float32
BF16 = jnp.bfloat16


def halves(table):
    high = np.asarray(table, np.float32).astype(jnp.bfloat16)
    low = (np.asarray(table, np.float64) - high.astype(np.float64)).astype(np.float32)
    return high, low.astype(jnp.bfloat16)


def offset_tables():
    forward, inverse = [], []
    place = np.arange(128)
    for p in range(2):
        wave = 2 * (np.arange(128) - 64) + p
        angle = 2.0 * np.pi * (np.outer(wave, place) % NH) / NH
        cos, sin = np.cos(angle), np.sin(angle)
        forward.append(np.block([[cos, sin], [-sin, cos]]))
        inverse.append(np.block([[cos.T, -sin.T], [sin.T, cos.T]]) / NH)
    return halves(np.stack(forward)), halves(np.stack(inverse))


def midpoint_tables():
    inner = np.arange(128)
    wave = (np.arange(128) + 64) % 128
    angle = 2.0 * np.pi * (np.outer(inner, wave) % 128) / 128
    cos, sin = np.cos(angle), np.sin(angle)
    forward = np.block([[cos, -sin], [sin, cos]])
    inverse = np.block([[cos.T, sin.T], [-sin.T, cos.T]]) / NM
    turn = 2.0 * np.pi * np.outer(np.arange(16), inner) / NM
    twiddle = np.stack([np.cos(turn), np.sin(turn)], 1)
    twiddle = np.broadcast_to(twiddle[:, :, None], (16, 2, 8, 128)).astype(np.float32)
    return halves(forward), halves(inverse), np.ascontiguousarray(twiddle)


def split(x):
    high = x.astype(BF16)
    return high, (x - high.astype(F32)).astype(BF16)


def dot(a, b):
    return jnp.dot(a, b, preferred_element_type=F32)


def dot_table_left(high, low, x):
    x_high, x_low = split(x)
    return dot(high, x_high) + (dot(high, x_low) + dot(low, x_high))


def dot_table_right(x, high, low):
    x_high, x_low = split(x)
    return dot(x_high, high) + (dot(x_low, high) + dot(x_high, low))


def times_root(value, step, sign):
    real, imag = value
    step = step % 16
    if step == 0:
        return value
    if step == 4:
        return (-imag * sign, real * sign)
    half = float(np.sqrt(0.5))
    if step == 2:
        return ((real - sign * imag) * half, (imag + sign * real) * half)
    if step == 6:
        return ((-real - sign * imag) * half, (-imag + sign * real) * half)
    c, s = math.cos(2 * math.pi * step / 16), sign * math.sin(2 * math.pi * step / 16)
    return (real * c - imag * s, real * s + imag * c)


def small_fft(values, sign):
    n = len(values)
    if n == 1:
        return values
    even, odd = small_fft(values[0::2], sign), small_fft(values[1::2], sign)
    odd = [times_root(v, k * (16 // n), sign) for k, v in enumerate(odd)]
    return [(e[0] + o[0], e[1] + o[1]) for e, o in zip(even, odd)] + [
        (e[0] - o[0], e[1] - o[1]) for e, o in zip(even, odd)
    ]


def place_here():
    return lax.axis_index("mid"), lax.axis_index("off")


def wait_bytes(ref, sem):
    pltpu.make_async_copy(ref, ref, sem).wait()


def code(values, peak):
    return jnp.round(values * (LEVELS / peak)).astype(jnp.int32).astype(jnp.int16)


def decode(codes, scale):
    return codes.astype(jnp.int32).astype(F32) * scale


def peak_of(arrays):
    top = functools.reduce(jnp.maximum, [jnp.abs(a) for a in arrays])
    return jnp.maximum(jnp.max(top, axis=0, keepdims=True), 1e-30)


def one_way(omega_sq, steps):
    wave = steps.astype(F32) * (math.pi / NM)
    level = omega_sq - wave * wave
    magnitude = jnp.sqrt(level * level + DAMP * DAMP)
    larger = jnp.sqrt(0.5 * (magnitude + jnp.abs(level)))
    smaller = DAMP / (2.0 * larger)
    real = jnp.where(level >= 0, larger, smaller)
    imag = jnp.where(level >= 0, smaller, larger)
    decay = jnp.exp(-DZ * imag)
    return decay * jnp.cos(DZ * real), decay * jnp.sin(DZ * real)


def slow_tile(layers_ref, slowness_ref, step, c):
    at = lax.broadcasted_iota(jnp.int32, (8, 128), 0)
    tile = jnp.zeros((8, 128), F32)
    for h in range(8):
        tile = jnp.where(at == h, slowness_ref[step, layers_ref[step, c, h]], tile)
    return tile


def frequency(index):
    return math.pi * (0.1 + 0.8 * (index.astype(F32) + 0.5) / NF)


def fill_phase(phase, omega, core):
    shape = (8, 256)
    i = lax.broadcasted_iota(jnp.int32, shape, 0)
    x = lax.broadcasted_iota(jnp.int32, shape, 1)
    omega_sq = omega * omega

    def one(k, _):
        mr, mi = one_way(omega_sq, k - 8 * core - NM + 16 * (x - i))
        pr, pi = one_way(omega_sq, k + 8 * core - NM + 16 * (x + i))
        for q in range(16):
            low = slice(128 - 8 * q, 256 - 8 * q)
            high = slice(8 * q, 8 * q + 128)
            ar, ai, br, bi = mr[:, low], mi[:, low], pr[:, high], pi[:, high]
            phase[0, k, 8 * q : 8 * q + 8, :] = ar * br - ai * bi
            phase[1, k, 8 * q : 8 * q + 8, :] = ar * bi + ai * br
        return 0

    lax.fori_loop(0, 16, one, 0)


def midpoint_chunk(x_ref, core, store, phase, tw_ref, fwd, inv, work, at):
    for sub in range(4):
        rows = pl.ds(at + sub * 8, 8)
        values = [
            (x_ref[a % 2, core, 0, a // 2, rows, :], x_ref[a % 2, core, 1, a // 2, rows, :])
            for a in range(16)
        ]
        for k, (real, imag) in enumerate(small_fft(values, -1)):
            cos, sin = tw_ref[k, 0], tw_ref[k, 1]
            here = pl.ds(k * 32 + sub * 8, 8)
            work[here, 0:128] = real * cos + imag * sin
            work[here, 128:256] = imag * cos - real * sin
    for part in range(4):
        here = pl.ds(part * 128, 128)
        z = dot_table_right(work[here, :], fwd[0][...], fwd[1][...])
        real, imag = z[:, :128], z[:, 128:]
        ks = pl.ds(part * 4, 4)
        turn_r = phase[0, ks, pl.ds(at, 32), :].reshape(128, 128)
        turn_i = phase[1, ks, pl.ds(at, 32), :].reshape(128, 128)
        z = jnp.concatenate(
            [real * turn_r - imag * turn_i, real * turn_i + imag * turn_r], axis=1
        )
        work[here, :] = dot_table_right(z, inv[0][...], inv[1][...])
    for sub in range(4):
        values = []
        for k in range(16):
            here = pl.ds(k * 32 + sub * 8, 8)
            real, imag = work[here, 0:128], work[here, 128:256]
            cos, sin = tw_ref[k, 0], tw_ref[k, 1]
            values.append((real * cos - imag * sin, real * sin + imag * cos))
        store(sub, small_fft(values, 1))


def field_kernel(
    targets_ref,
    counts_ref,
    layers_ref,
    slowness_ref,
    bins_hbm,
    ops_hbm,
    *rest,
):
    tables_hbm, (z_ref, zs_ref, turn_ref), scratch = rest[:9], rest[9:12], rest[12:]
    field_body(
        targets_ref,
        counts_ref,
        layers_ref,
        slowness_ref,
        (bins_hbm, ops_hbm, *tables_hbm),
        scratch[:11],
        z_ref,
        zs_ref,
        turn_ref,
        *scratch[11:],
    )


def field_body(
    targets_ref,
    counts_ref,
    layers_ref,
    slowness_ref,
    held_far,
    held_near,
    z_ref,
    zs_ref,
    turn_ref,
    row_ref,
    slow_ref,
    made,
    sent,
    sent_s,
    held,
    held_s,
    rows,
    slows,
    turns,
    phase,
    w_high,
    w_low,
    both_high,
    both_low,
    folded,
    x0,
    d0,
    x1,
    work,
    chunk_out,
    coded,
    coded_s,
    ssem,
    rsem,
    msem,
    pair_s,
    pair_r,
    load_sem,
    last_turns,
):
    bins_ref, ops_ref, oh_ref, ol_ref, gh_ref, gl_ref, fh, fl, ih, il, tw_ref = held_near
    loads = [
        pltpu.make_async_copy(far, near, load_sem.at[i])
        for i, (far, near) in enumerate(zip(held_far, held_near))
    ]
    j, o = place_here()
    core, group = lax.rem(o, 2), o // 2
    partner = o + 1 - 2 * core
    me, total = j * OFF + o, MID * OFF
    barrier = pltpu.get_barrier_semaphore()

    def signal(i, _):
        peer = lax.rem(me + i, total)
        pl.semaphore_signal(
            barrier, inc=1, device_id=(peer // OFF, lax.rem(peer, OFF)), device_id_type=MESH
        )
        return 0

    for load in loads[:2]:
        load.start()
    lax.fori_loop(1, total, signal, 0)
    for load in loads[2:]:
        load.start()

    for load in loads[:2]:
        load.wait()
    for c in range(2):
        source = bins_ref[0, :, :, c * BLK : (c + 1) * BLK].reshape(2 * NF, BLK)
        for e in range(0, ENT, 2):
            out = dot(source, jnp.concatenate([ops_ref[0, e], ops_ref[0, e + 1]], axis=1))
            made[c, pl.ds(e * 128, 128), :] = out[:, :BLK]
            made[c, pl.ds(e * 128 + 128, 128), :] = out[:, BLK:]

    lane = lax.broadcasted_iota(jnp.int32, (ENT, NB * ENT), 1)
    spread = (lax.rem(lane, ENT) == lax.broadcasted_iota(jnp.int32, lane.shape, 0)).astype(F32)
    found = dot(
        jnp.broadcast_to((targets_ref[...] + 1).astype(F32), (8, ENT)).astype(BF16),
        spread.astype(BF16),
    )[:1]
    slot = lax.broadcasted_iota(jnp.int32, (1, NB * ENT), 1)
    live = (slot // ENT == o) & (lax.rem(slot, ENT) < counts_ref[0])
    row_ref[...] = jnp.where(live, found, 0.0)
    for c in range(2):
        slow_ref[c] = slow_tile(layers_ref, slowness_ref, 0, c)

    pl.semaphore_wait(barrier, total - 1)

    pltpu.make_async_copy(row_ref, rows.at[o], msem.at[0]).start()
    pltpu.make_async_copy(slow_ref, slows.at[j], msem.at[1]).start()

    def send_row(i, _):
        peer = lax.rem(o + i, OFF)
        pltpu.make_async_remote_copy(
            row_ref, rows.at[o], msem.at[2], msem.at[0], device_id=(j, peer), device_id_type=MESH
        ).start()
        return 0

    lax.fori_loop(1, OFF, send_row, 0)

    def send_slow(i, _):
        peer = lax.rem(j + i, MID)
        pltpu.make_async_remote_copy(
            slow_ref, slows.at[j], msem.at[3], msem.at[1], device_id=(peer, o), device_id_type=MESH
        ).start()
        return 0

    lax.fori_loop(1, MID, send_slow, 0)

    x_at, y_at, z_at = j // 2, 2 * lax.rem(j, 2) + lax.rem(o // 2, 2), o // 4

    def peer_at(classes, i):
        there, rest = [], i // 2
        for at, distance in zip((x_at, y_at, z_at), classes):
            step = 1 + 2 * lax.rem(rest, 2) if distance == 1 else distance
            rest = rest // 2 if distance == 1 else rest
            there.append(lax.rem(at + step, 4))
        x, y, z = there
        return 2 * x + y // 2, 4 * z + 2 * lax.rem(y, 2) + lax.rem(core + i, 2)

    def encode(peer_j, peer_o):
        f, c = 8 * (peer_o // 2) + peer_j, lax.rem(peer_o, 2)
        values = [made[c, pl.ds(2 * f + part, ENT, stride=2 * NF), :] for part in range(2)]
        peak = peak_of(values)
        for part in range(2):
            sent[peer_j, peer_o, part] = code(values[part], peak)
        sent_s[peer_j, peer_o] = peak * (1.0 / LEVELS)

    def send(peer_j, peer_o):
        for source, target, at in ((sent, held, 0), (sent_s, held_s, 1)):
            pltpu.make_async_remote_copy(
                source.at[peer_j, peer_o],
                target.at[j, o],
                ssem.at[at],
                rsem.at[at],
                device_id=(peer_j, peer_o),
                device_id_type=MESH,
            ).start()

    for classes in sorted(itertools.product(range(3), repeat=3), key=lambda d: -sum(d)):
        first = 0 if any(classes) else 1
        members = 2 ** (1 + classes.count(1))

        def encode_one(i, _, classes=classes):
            encode(*peer_at(classes, i))
            return 0

        def send_one(i, _, classes=classes):
            send(*peer_at(classes, i))
            return 0

        lax.fori_loop(0, members, encode_one, 0, unroll=2)
        lax.fori_loop(first, members, send_one, 0)
    pltpu.make_async_copy(sent.at[j, o], held.at[j, o], rsem.at[0]).start()
    pltpu.make_async_copy(sent_s.at[j, o], held_s.at[j, o], rsem.at[1]).start()

    for load in loads[2:]:
        load.wait()

    own_f = lax.broadcasted_iota(jnp.int32, (8, 128), 0) * 0 + (group * MID + j)
    omega = frequency(own_f)
    fill_phase(phase, jnp.concatenate([omega, omega], axis=1), core)
    for c in range(2):
        slow = slow_tile(layers_ref, slowness_ref, 1, c)
        for f in range(4):
            last_f = lax.broadcasted_iota(jnp.int32, (8, 128), 0) * 0 + (o * 4 + f)
            turn = 2.0 * DZ * frequency(last_f) * (slow - 1.0)
            last_turns[f, c, 0] = jnp.cos(turn)
            last_turns[f, c, 1] = jnp.sin(turn)
    give_turns = pltpu.make_async_copy(last_turns, turn_ref, load_sem.at[11])
    give_turns.start()
    wait_bytes(slows, msem.at[1])
    for jm in range(MID):
        turn = 2.0 * DZ * omega * (slows[jm, core] - 1.0)
        turns[jm, 0] = jnp.cos(turn)
        turns[jm, 1] = jnp.sin(turn)
    wait_bytes(rows, msem.at[0])
    target = jnp.sum(rows[:, 0, :], axis=0, keepdims=True).astype(jnp.int32) - 1
    spot = lax.broadcasted_iota(jnp.int32, (128, NB * ENT), 0)
    first, second = (spot == target).astype(F32), (spot + 128 == target).astype(F32)
    for p in range(2):
        pick = ((first + second) if p == 0 else (first - second)).astype(BF16)
        for part in range(2):
            cols = pl.ds(part * 128, 128)
            at = pl.ds(part * NH, NH)
            w_high[p, :, at] = dot(oh_ref[p, :, cols], pick).astype(BF16)
            w_low[p, :, at] = dot(ol_ref[p, :, cols], pick).astype(BF16)
    wait_bytes(rows.at[pl.ds(0, OFF - 1)], msem.at[2])
    wait_bytes(slows.at[pl.ds(0, MID - 1)], msem.at[3])
    wait_bytes(held_s, rsem.at[1])
    wait_bytes(held, rsem.at[0])

    def pair_copy(ref, pair, step):
        here = ref.at[core, 1 - core, :, pl.ds(2 * pair, 2)]
        return pltpu.make_async_remote_copy(
            here,
            here,
            pair_s.at[step, pair],
            pair_r.at[step, pair],
            device_id=(j, partner),
            device_id_type=MESH,
        )

    def put_waves(ref, pair, p, out):
        for q in range(2):
            for part in range(2):
                ref[core, p, part, 2 * pair + q] = out[
                    part * 128 : (part + 1) * 128, q * 128 : (q + 1) * 128
                ]

    def slots_to_waves(x_high, x_low, p):
        high, low = w_high[p], w_low[p]
        return dot(high, x_high) + (dot(high, x_low) + dot(low, x_high))

    def to_waves(pair, _):
        both = jnp.concatenate(
            [
                jnp.concatenate(
                    [
                        decode(held[2 * pair + q, :, part], held_s[2 * pair + q]).reshape(
                            NB * ENT, 128
                        )
                        for q in range(2)
                    ],
                    axis=1,
                )
                for part in range(2)
            ],
            axis=0,
        )
        x_high, x_low = split(both)
        both_high[pair], both_low[pair] = x_high, x_low
        put_waves(x0, pair, 1 - core, slots_to_waves(x_high, x_low, 1 - core))
        pair_copy(x0, pair, 0).start()
        return 0

    def to_own_waves(pair, _):
        put_waves(x0, pair, core, slots_to_waves(both_high[pair], both_low[pair], core))
        return 0

    lax.fori_loop(0, MID // 2, to_waves, 0)
    lax.fori_loop(0, MID // 2, to_own_waves, 0)
    for pair in range(MID // 2):
        pair_copy(x0, pair, 0).wait_recv()

    def chunk_copy(i):
        here = d0.at[core, 1 - core, :, :, pl.ds(pl.multiple_of(i * 32, 32), 32)]
        return pltpu.make_async_remote_copy(
            here,
            here,
            pair_s.at[1, i],
            pair_r.at[1, i],
            device_id=(j, partner),
            device_id_type=MESH,
        )

    def first_chunk(i, _):
        at = pl.multiple_of(i * 32, 32)

        def store(sub, values):
            rows_here = pl.ds(at + sub * 8, 8)
            for a, (real, imag) in enumerate(values):
                d0[core, a % 2, 0, a // 2, rows_here, :] = real
                d0[core, a % 2, 1, a // 2, rows_here, :] = imag

        midpoint_chunk(x0, core, store, phase, tw_ref, (fh, fl), (ih, il), work, at)
        chunk_copy(i).start()
        return 0

    lax.fori_loop(0, 4, first_chunk, 0)
    for i in range(4):
        chunk_copy(i).wait_recv()

    own_sign = (1 - 2 * core).astype(F32)

    def space(pair, _):
        fields = []
        for p in range(2):
            both = jnp.concatenate(
                [
                    jnp.concatenate([d0[p, core, part, 2 * pair + q] for q in range(2)], axis=1)
                    for part in range(2)
                ],
                axis=0,
            )
            fields.append(dot_table_left(gh_ref[p], gl_ref[p], both))
        ends = [fields[0] + fields[1], fields[0] - fields[1]]
        for end in range(2):
            turned = []
            for q in range(2):
                cos, sin = turns[2 * pair + q, 0], turns[2 * pair + q, 1]
                lanes = slice(q * 128, (q + 1) * 128)
                out_r, out_i = [], []
                for h in range(4):
                    real = ends[end][h * 32 : (h + 1) * 32, lanes]
                    imag = ends[end][128 + h * 32 : 128 + (h + 1) * 32, lanes]
                    at = 4 * end + h
                    c, s = cos[at : at + 1], sin[at : at + 1]
                    out_r.append(real * c - imag * s)
                    out_i.append(real * s + imag * c)
                turned.append(jnp.concatenate(out_r + out_i, axis=0))
            ends[end] = jnp.concatenate(turned, axis=1)
        folded[pair] = ends[0] + own_sign * ends[1]
        other = dot_table_left(
            oh_ref[1 - core], ol_ref[1 - core], ends[0] - own_sign * ends[1]
        )
        put_waves(x1, pair, 1 - core, other)
        pair_copy(x1, pair, 2).start()
        return 0

    def own_space(pair, _):
        put_waves(x1, pair, core, dot_table_left(oh_ref[core], ol_ref[core], folded[pair]))
        return 0

    lax.fori_loop(0, MID // 2, space, 0, unroll=2)
    lax.fori_loop(0, MID // 2, own_space, 0, unroll=2)
    for pair in range(MID // 2):
        pair_copy(x1, pair, 2).wait_recv()

    owner, mine = j // 4, lax.rem(j, 4)
    stays = owner == core
    half_at = lax.rem(j, 2)

    def deliver(peer, i, near):
        for source, target, at in ((coded, z_ref, 2), (coded_s, zs_ref, 3)):
            here, there = source.at[peer, i], target.at[mine, core, i]
            if near:
                pltpu.make_async_copy(here, there, rsem.at[at]).start()
            else:
                pltpu.make_async_remote_copy(
                    here,
                    there,
                    ssem.at[at],
                    rsem.at[at],
                    device_id=(peer, 2 * group + owner),
                    device_id_type=MESH,
                ).start()

    def second_chunk(i, _):
        at = pl.multiple_of(i * 32, 32)

        def store(sub, values):
            rows_here = pl.ds(sub * 8, 8)
            for a, (real, imag) in enumerate(values):
                chunk_out[a // 2, a % 2, 0, rows_here, :] = real
                chunk_out[a // 2, a % 2, 1, rows_here, :] = imag

        midpoint_chunk(x1, core, store, phase, tw_ref, (fh, fl), (ih, il), work, at)

        def encode_peer(peer, _):
            for c in range(2):
                values = [chunk_out[peer, c, part] for part in range(2)]
                peak = peak_of(values)
                for part in range(2):
                    coded[peer, i, c, part] = code(values[part], peak)
                coded_s[peer, i, c] = peak * (1.0 / LEVELS)
            return 0

        lax.fori_loop(0, MID, encode_peer, 0)
        for dx, dy in ((2, 1), (1, 1), (3, 1), (0, 1), (2, 0), (1, 0), (3, 0)):
            peer = 2 * lax.rem(x_at + dx, 4) + lax.rem(half_at + dy, 2)
            deliver(peer, i, False)

        @pl.when(stays)
        def _():
            deliver(j, i, True)

        @pl.when(jnp.logical_not(stays))
        def _():
            deliver(j, i, False)

        return 0

    lax.fori_loop(0, 4, second_chunk, 0)

    give_turns.wait()
    for at, ref in ((0, sent), (1, sent_s)):
        wait_bytes(ref.at[0, pl.ds(0, OFF - 1)], ssem.at[at])
        wait_bytes(ref.at[pl.ds(1, MID - 1)], ssem.at[at])
    for i in range(4):
        pair_copy(x0, i, 0).wait_send()
        chunk_copy(i).wait_send()
        pair_copy(x1, i, 2).wait_send()
    for at, ref in ((2, coded), (3, coded_s)):
        wait_bytes(ref.at[pl.ds(0, MID - 1)], ssem.at[at])

        @pl.when(jnp.logical_not(stays))
        def _():
            wait_bytes(ref.at[0], ssem.at[at])

    wait_bytes(zs_ref, rsem.at[3])
    wait_bytes(z_ref, rsem.at[2])


HALVES = (2, 2, 2, MID, 128, 128)


def propagate(*args):
    return pl.pallas_call(
        field_kernel,
        out_shape=[
            jax.ShapeDtypeStruct((4, 2, 4, 2, 2, 32, 128), jnp.int16),
            jax.ShapeDtypeStruct((4, 2, 4, 2, 1, 128), F32),
            jax.ShapeDtypeStruct((4, 2, 2, 8, 128), F32),
        ],
        in_specs=[VM] + [SM] * 3 + [ANY] * (len(args) - 4),
        out_specs=[ANY] * 3,
        scratch_shapes=[pltpu.VMEM(a.shape, a.dtype) for a in args[4:]]
        + [
            pltpu.VMEM((1, NB * ENT), F32),
            pltpu.VMEM((2, 8, 128), F32),
            pltpu.VMEM((2, ENT * 2 * NF, BLK), F32),
            pltpu.VMEM((MID, OFF, 2, ENT, BLK), jnp.int16),
            pltpu.VMEM((MID, OFF, 1, BLK), F32),
            pltpu.VMEM((MID, NB, 2, ENT, BLK), jnp.int16),
            pltpu.VMEM((MID, NB, 1, BLK), F32),
            pltpu.VMEM((NB, 1, NB * ENT), F32),
            pltpu.VMEM((MID, 2, 8, 128), F32),
            pltpu.VMEM((MID, 2, 8, 128), F32),
            pltpu.VMEM((2, 16, 128, 128), F32),
            pltpu.VMEM((2, 256, 512), BF16),
            pltpu.VMEM((2, 256, 512), BF16),
            pltpu.VMEM((4, 512, 256), BF16),
            pltpu.VMEM((4, 512, 256), BF16),
            pltpu.VMEM((4, 256, 256), F32),
            pltpu.VMEM(HALVES, F32),
            pltpu.VMEM(HALVES, F32),
            pltpu.VMEM(HALVES, F32),
            pltpu.VMEM((512, 256), F32),
            pltpu.VMEM((MID, 2, 2, 32, 128), F32),
            pltpu.VMEM((MID, 4, 2, 2, 32, 128), jnp.int16),
            pltpu.VMEM((MID, 4, 2, 1, 128), F32),
            pltpu.SemaphoreType.DMA((4,)),
            pltpu.SemaphoreType.DMA((4,)),
            pltpu.SemaphoreType.DMA((4,)),
            pltpu.SemaphoreType.DMA((3, 4)),
            pltpu.SemaphoreType.DMA((3, 4)),
            pltpu.SemaphoreType.DMA((12,)),
            pltpu.VMEM((4, 2, 2, 8, 128), F32),
        ],
        compiler_params=pltpu.CompilerParams(
            collective_id=0, has_side_effects=True, vmem_limit_bytes=56 << 20
        ),
        name="propagate",
    )(*args)


def last_kernel(z_ref, zs_ref, turn_ref, gh_ref, gl_ref, out_ref):
    fields = []
    for p in range(2):
        both = jnp.concatenate(
            [
                jnp.concatenate(
                    [decode(z_ref[0, p, q, c, part], zs_ref[0, p, q, c]) for c in range(2)],
                    axis=1,
                )
                for part in range(2)
                for q in range(4)
            ],
            axis=0,
        )
        fields.append(dot_table_left(gh_ref[p], gl_ref[p], both))
    ends = [fields[0] + fields[1], fields[0] - fields[1]]
    for c in range(2):
        cos, sin = turn_ref[0, c, 0], turn_ref[0, c, 1]
        lanes = slice(c * 128, (c + 1) * 128)
        for h in range(8):
            end, at = ends[h // 4], (h % 4) * 32
            real, imag = end[at : at + 32, lanes], end[128 + at : 160 + at, lanes]
            co, si = cos[h : h + 1], sin[h : h + 1]
            for part, value in enumerate((real * co - imag * si, real * si + imag * co)):
                out_ref[0, pl.ds(128 * h + 2 * c + part, 32, stride=4), :] = value


def last(z, zs, turns, inv):
    whole = pl.BlockSpec((2, 256, 256), lambda i: (0, 0, 0))
    return pl.pallas_call(
        last_kernel,
        grid=(4,),
        out_shape=jax.ShapeDtypeStruct((4, NH * 4, 128), F32),
        in_specs=[
            pl.BlockSpec((1, 2, 4, 2, 2, 32, 128), lambda i: (i, 0, 0, 0, 0, 0, 0)),
            pl.BlockSpec((1, 2, 4, 2, 1, 128), lambda i: (i, 0, 0, 0, 0, 0)),
            pl.BlockSpec((1, 2, 2, 8, 128), lambda i: (i, 0, 0, 0, 0)),
            whole,
            whole,
        ],
        out_specs=pl.BlockSpec((1, NH * 4, 128), lambda i: (i, 0, 0)),
        compiler_params=pltpu.CompilerParams(vmem_limit_bytes=56 << 20),
        name="last_offsets",
    )(z, zs, turns, *inv)


def local(bins_data, operators, targets, counts, layer_index, slowness):
    (forward, inverse), (mid_fwd, mid_inv, twiddle) = offset_tables(), midpoint_tables()
    layers = layer_index.transpose(0, 2, 1)
    z, zs, turns = propagate(
        targets,
        counts,
        layers,
        slowness,
        bins_data,
        operators,
        *forward,
        *inverse,
        *mid_fwd,
        *mid_inv,
        twiddle,
    )
    rows = last(z, zs, turns, inverse)
    return rows.reshape(4, NH, 2, 2, 128).transpose(0, 1, 3, 2, 4).reshape(4, NH, 2, 256)


def solution(mesh):
    in_specs = (
        P("off", None, None, "mid"),
        P("off", None, None, None),
        P("off", None),
        P("off"),
        P(None, None, "mid"),
        P(),
    )
    out_specs = P("off", None, None, "mid")
    return jax.shard_map(local, mesh=mesh, in_specs=in_specs, out_specs=out_specs, check_vma=False)
```
